32 devices in a mesh: sim: 2 (over y), slab: 16 (over z, x, core).
Axes of the slice: x: 2, y: 2, z: 4, core: 2. Of those that a mesh axis runs over, the one named last changes fastest.
Arguments:
- velocity: float32 [2, 3, 256, 256, 128], P('sim', None, None, 'slab'), may hold values from -3 to 5
- viscosity: float32 [2, 256, 256, 128], P('sim', None, 'slab'), may hold values from 0.02 to 0.12
- turbines: int32 [2, 256, 256, 128], P('sim', None, 'slab'), may hold values from 0 to 1, as said below
- fringe_start: int32 [1], replicated, may hold values from 0 to 224
Outputs:
- projected: float32 [2, 3, 256, 256, 128], P('sim', None, None, 'slab')
The draws below stay inside these ranges and needn't reach their ends.
Inputs may be any that keep to these rules, and one draw needn't show every extreme that they name: `turbines`: group 0, the precursor, holds no turbine cells.
All inputs are finite; a program needn't handle non-finite values.
Results may differ from the reference program's by a relative error of at most 0.0003.
Values sent between devices are 32-bit elements; how exact they have to be, the bound alone decides.
A program may use at most 128 MiB of HBM per device.

```python
import math
import jax
import jax.numpy as jnp
from jax import lax

NX = 256
NY = 256
NZ = 128
FR = 32
STEPS = 1
GROUPS = 2


def draw_velocity(key, part):
    noise_key = jax.random.fold_in(jax.random.fold_in(key, 11), 0)
    full_shape = (GROUPS, 3, NX, NY, NZ)
    turbulence = jax.random.normal(noise_key, full_shape, jnp.float32)
    mean_flow = jnp.array([1.0, 0.0, 0.0], jnp.float32).reshape(1, 3, 1, 1, 1)
    values = 0.5 * turbulence + mean_flow
    return jnp.clip(values, -3.0, 5.0)


def draw_turbines(key, part):
    key_x, key_y, key_z = jax.random.split(jax.random.fold_in(key, 23), 3)
    machines = 12
    column_x = jax.random.randint(key_x, (GROUPS, machines), 0, NX)
    column_y = jax.random.randint(key_y, (GROUPS, machines), 0, NY)
    height_z = jax.random.randint(key_z, (GROUPS, machines), NZ // 4, NZ // 2 + 1)
    radius = max(NZ // 8, 1)
    along_x = jnp.arange(NX, dtype=jnp.int32).reshape(1, NX, 1, 1)
    along_y = jnp.arange(NY, dtype=jnp.int32).reshape(1, 1, NY, 1)
    along_z = jnp.arange(NZ, dtype=jnp.int32).reshape(1, 1, 1, NZ)
    disc_mask = jnp.zeros((GROUPS, NX, NY, NZ), jnp.int32)
    for machine in range(machines):
        centre_x = column_x[:, machine].reshape(GROUPS, 1, 1, 1)
        centre_y = column_y[:, machine].reshape(GROUPS, 1, 1, 1)
        centre_z = height_z[:, machine].reshape(GROUPS, 1, 1, 1)
        inside = (along_x == centre_x) & ((along_y - centre_y) ** 2 + (along_z - centre_z) ** 2 <= radius * radius)
        disc_mask = jnp.maximum(disc_mask, inside.astype(jnp.int32))
    group_ids = jnp.arange(GROUPS, dtype=jnp.int32).reshape(GROUPS, 1, 1, 1)
    return jnp.where(group_ids == 0, 0, disc_mask)


def steps_of(stream_key, dims, cuts, smallest, top_value):
    loudness = 1.0
    for axis_at, shards_of in cuts:
        draws = jax.random.uniform(jax.random.fold_in(jax.random.fold_in(stream_key, 6), axis_at), (shards_of,), jnp.float32, smallest / len(cuts), top_value / len(cuts))
        loudness = loudness * jnp.repeat(jnp.exp(draws), dims[axis_at] // shards_of).reshape((-1,) + (1,) * (len(dims) - 1 - axis_at))
    return loudness


def setup_inputs(seed: int = 0) -> dict:
    keys = jax.random.split(jax.random.key(seed), 5)
    velocity = draw_velocity(jax.random.fold_in(keys[4], 71), 0)
    viscosity = jnp.clip(jnp.exp(math.log(0.12) - 1.7917595 * jax.random.uniform(keys[1], (GROUPS, NX, NY, NZ), jnp.float32) ** steps_of(keys[1], (GROUPS, NX, NY, NZ), ((0, 2), (2, 16)), -0.2, 0.2)), 0.02, 0.12)
    turbines = draw_turbines(jax.random.fold_in(keys[4], 71), 0)
    fringe_start = jax.random.randint(keys[3], (1,), 0, NX - FR + 1).astype(jnp.int32)
    return dict(velocity=velocity, viscosity=viscosity, turbines=turbines, fringe_start=fringe_start)


highest = lax.Precision.HIGHEST
thrust_coef = 0.75


def wrap_y(values):
    return jnp.concatenate([values[..., -1:, :], values, values[..., :1, :]], -2)


def diffuse(fields, viscous):
    faces_x = 0.5 * (viscous + jnp.roll(viscous, -1, -3))
    flux_x = faces_x * (jnp.roll(fields, -1, -3) - fields)
    across_x = flux_x - jnp.roll(flux_x, 1, -3)
    faces_y = 0.5 * (viscous[..., 1:, :] + viscous[..., :-1, :])
    flux_y = faces_y * (fields[..., 1:, :] - fields[..., :-1, :])
    across_y = flux_y[..., 1:, :] - flux_y[..., :-1, :]
    faces_z = 0.5 * (viscous[..., 1:] + viscous[..., :-1])
    flux_z = faces_z * (fields[..., 1:] - fields[..., :-1])
    nothing = jnp.zeros_like(flux_z[..., :1])
    upper_flux = jnp.concatenate([flux_z, nothing], -1)
    lower_flux = jnp.concatenate([nothing, flux_z], -1)
    across_z = upper_flux - lower_flux
    return fields[..., 1:-1, :] + across_x[..., 1:-1, :] + across_y + across_z[..., 1:-1, :]


def drag(fields, turbine_cells):
    streamwise = fields[0]
    disc_mask = turbine_cells.astype(jnp.float32)
    streamwise = streamwise - 0.5 * thrust_coef * disc_mask * streamwise * jnp.abs(streamwise)
    return jnp.concatenate([streamwise[None], fields[1:]], 0)


def blend_rows(fields, precursor, first_row, active):
    length = precursor.shape[1]
    slab_rows = lax.dynamic_slice_in_dim(fields, first_row, length, 1)
    profile = jnp.sin(math.pi * (jnp.arange(length, dtype=jnp.float32) + 0.5) / length) ** 2 * active
    new_rows = slab_rows + profile[None, :, None, None] * (precursor - slab_rows)
    return lax.dynamic_update_slice_in_dim(fields, new_rows, first_row, 1)


def centered_x(values):
    return 0.5 * (jnp.roll(values, -1, -3) - jnp.roll(values, 1, -3))


def centered_y(extended):
    return 0.5 * (extended[..., 2:, :] - extended[..., :-2, :])


def centered_z(values):
    padded = jnp.concatenate([values[..., :1], values, values[..., -1:]], -1)
    return 0.5 * (padded[..., 2:] - padded[..., :-2])


def dft_tables(length):
    index_a = jnp.arange(length, dtype=jnp.int32)
    product = (index_a[:, None] * index_a[None, :]) % length
    angles = (2.0 * math.pi / length) * product.astype(jnp.float32)
    return jnp.cos(angles), jnp.sin(angles)


def dct_table(length):
    index_m = jnp.arange(length, dtype=jnp.int32)
    product = (index_m[:, None] * (2 * index_m[None, :] + 1)) % (4 * length)
    angles = (math.pi / (2.0 * length)) * product.astype(jnp.float32)
    return jnp.cos(angles)


def inverse_eigen(wave_x, wave_y, wave_z, length_x, length_y, length_z):
    eigen_x = 2.0 * jnp.cos(2.0 * math.pi * wave_x.astype(jnp.float32) / length_x) - 2.0
    eigen_y = 2.0 * jnp.cos(2.0 * math.pi * wave_y.astype(jnp.float32) / length_y) - 2.0
    eigen_z = 2.0 * jnp.cos(math.pi * wave_z.astype(jnp.float32) / length_z) - 2.0
    eigen_sum = eigen_x[:, None, None] + eigen_y[None, :, None] + eigen_z[None, None, :]
    zero_mode = (wave_x[:, None, None] == 0) & (wave_y[None, :, None] == 0) & (wave_z[None, None, :] == 0)
    guarded = jnp.where(zero_mode, 1.0, eigen_sum)
    return jnp.where(zero_mode, 0.0, 1.0 / guarded)


def poisson(source):
    cos_x, sin_x = dft_tables(NX)
    cos_y, sin_y = dft_tables(NY)
    cos_z = dct_table(NZ)
    z_modes = jnp.einsum("xyn,mn->xym", source, cos_z, precision=highest)
    real_part = jnp.einsum("kx,xyz->kyz", cos_x, z_modes, precision=highest)
    imag_part = -jnp.einsum("kx,xyz->kyz", sin_x, z_modes, precision=highest)
    y_real = jnp.einsum("ky,xyz->xkz", cos_y, real_part, precision=highest) + jnp.einsum("ky,xyz->xkz", sin_y, imag_part, precision=highest)
    y_imag = jnp.einsum("ky,xyz->xkz", cos_y, imag_part, precision=highest) - jnp.einsum("ky,xyz->xkz", sin_y, real_part, precision=highest)
    inverse = inverse_eigen(jnp.arange(NX, dtype=jnp.int32), jnp.arange(NY, dtype=jnp.int32), jnp.arange(NZ, dtype=jnp.int32), NX, NY, NZ)
    press_real = y_real * inverse
    press_imag = y_imag * inverse
    back_real = (jnp.einsum("ky,xyz->xkz", cos_y, press_real, precision=highest) - jnp.einsum("ky,xyz->xkz", sin_y, press_imag, precision=highest)) / NY
    back_imag = (jnp.einsum("ky,xyz->xkz", sin_y, press_real, precision=highest) + jnp.einsum("ky,xyz->xkz", cos_y, press_imag, precision=highest)) / NY
    spatial_x = (jnp.einsum("xk,kyz->xyz", cos_x, back_real, precision=highest) - jnp.einsum("xk,kyz->xyz", sin_x, back_imag, precision=highest)) / NX
    weights = jnp.where(jnp.arange(NZ, dtype=jnp.int32) == 0, 1.0, 2.0) / NZ
    return jnp.einsum("xym,mn->xyn", spatial_x, cos_z * weights[:, None], precision=highest)


def reference(velocity, viscosity, turbines, fringe_start):
    first_row = fringe_start[0]
    precursor = lax.dynamic_slice_in_dim(velocity[0], first_row, FR, 1)

    def one_group(group_index):
        fields = velocity[group_index]
        viscous = viscosity[group_index]
        for substep in range(STEPS):
            fields = diffuse(wrap_y(fields), wrap_y(viscous))
        fields = drag(fields, turbines[group_index])
        active = (group_index != 0).astype(jnp.float32)
        fields = blend_rows(fields, precursor, first_row, active)
        divergence = centered_x(fields[0]) + centered_y(wrap_y(fields[1])) + centered_z(fields[2])
        pressure = poisson(divergence)
        gradient = jnp.stack([centered_x(pressure), centered_y(wrap_y(pressure)), centered_z(pressure)])
        return fields - gradient

    return lax.map(one_group, jnp.arange(GROUPS, dtype=jnp.int32))
```

```python
import math

import jax
import jax.numpy as jnp
import numpy as np
from jax import lax
from jax.experimental import pallas as pl
from jax.experimental.pallas import tpu as pltpu
from jax.sharding import PartitionSpec as P

FR = 32

thrust_coef = 0.75
MESH = pl.DeviceIdType.MESH
VM = pltpu.VMEM
GRANT = 60 * 1024 * 1024


def dot(a, b):
    return jnp.dot(a, b, precision=lax.Precision.HIGHEST, preferred_element_type=jnp.float32)


def full(space=VM):
    return pl.BlockSpec(memory_space=space)


def tables(nx, ny, nz, rows):
    half = nx // 2
    wave = np.concatenate([np.arange(half), [half], np.arange(1, half)])
    at = np.arange(nx)
    angle = 2.0 * np.pi * ((wave[:, None] * at[None, :]) % nx) / nx
    is_sine = (np.arange(nx) > half)[:, None]
    fwd_x = np.where(is_sine, -np.sin(angle), np.cos(angle))
    weight = np.where((wave == 0) | (wave == half), 1.0, 2.0) / nx
    inv_x = (fwd_x * weight[:, None]).T
    m = np.arange(nz)
    cos_z = np.cos(np.pi * ((m[:, None] * (2 * m[None, :] + 1)) % (4 * nz)) / (2.0 * nz))
    inv_z = cos_z * (np.where(m == 0, 1.0, 2.0) / nz)[:, None]
    a = (4.0 * np.sin(np.pi * wave / nx) ** 2)[:, None] + (4.0 * np.sin(np.pi * m / (2.0 * nz)) ** 2)[None, :]
    root = np.sqrt(a + a * a / 4.0)
    mu = 1.0 / (1.0 + a / 2.0 + root)
    zero = a == 0.0
    coef = np.where(zero, 0.0, -1.0 / np.where(zero, 1.0, 2.0 * root))
    q = mu**rows
    wrap = 1.0 / np.where(zero, 1.0, 1.0 - mu**ny)
    f32 = lambda t: np.asarray(t, np.float32)
    return dict(fwd_x=f32(fwd_x), inv_x=f32(inv_x), fwd_z=f32(cos_z.T), inv_z=f32(inv_z), mu=f32(mu), coef=f32(coef), q=f32(q), wrap=f32(wrap))


def xroll(value, shift):
    return pltpu.roll(value, shift % value.shape[0], 0)


def zroll(value, shift):
    return pltpu.roll(value, shift % value.shape[1], 1)


def edges_kernel(rows, vel, visc, lo, hi):
    nx = lo.shape[1]
    for c in range(4):
        for at, out in ((0, lo), (rows - 1, hi)):
            pick = pl.ds(at, nx, stride=rows)
            out[c] = visc[pick, :] if c == 3 else vel[c, pick, :]


def halo_kernel(sims, slabs, lo, hi, fringe, left, right, pre, send, recv, psend, precv):
    sim, me = lax.axis_index("sim"), lax.axis_index("slab")
    after, before = lax.rem(me + 1, slabs), lax.rem(me + slabs - 1, slabs)
    barrier = pltpu.get_barrier_semaphore()
    for peer in (after, before):
        pl.semaphore_signal(barrier, inc=1, device_id=(sim, peer), device_id_type=MESH)

    @pl.when(sim == 0)
    def _():
        for other in range(1, sims):
            pl.semaphore_signal(barrier, inc=1, device_id=(other, me), device_id_type=MESH)

    @pl.when(sim != 0)
    def _():
        pl.semaphore_signal(barrier, inc=1, device_id=(0, me), device_id_type=MESH)

    @pl.when(sim == 0)
    def _():
        pl.semaphore_wait(barrier, 2 + sims - 1)

    @pl.when(sim != 0)
    def _():
        pl.semaphore_wait(barrier, 3)

    to_after = pltpu.make_async_remote_copy(hi, left, send.at[0], recv.at[0], device_id=(sim, after), device_id_type=MESH)
    to_before = pltpu.make_async_remote_copy(lo, right, send.at[1], recv.at[1], device_id=(sim, before), device_id_type=MESH)
    to_after.start()
    to_before.start()

    def share(other):
        return pltpu.make_async_remote_copy(fringe, pre, psend.at[other - 1], precv, device_id=(other, me), device_id_type=MESH)

    @pl.when(sim == 0)
    def _():
        for other in range(1, sims):
            share(other).start()

    to_after.wait()
    to_before.wait()

    @pl.when(sim == 0)
    def _():
        for other in range(1, sims):
            share(other).wait_send()
        pre[...] = fringe[...]

    @pl.when(sim != 0)
    def _():
        share(1).wait_recv()


def step_kernel(rows, start, vel, visc, turb, left, right, pre, prof, out, ext):
    nx = left.shape[1]
    for c in range(4):
        ext[c, 0] = left[c]
        ext[c, rows + 1] = right[c]

    @pl.loop(0, rows)
    def _(y):
        pick = pl.ds(y, nx, stride=rows)
        for c in range(3):
            ext[c, y + 1] = vel[c, pick, :]
        ext[3, y + 1] = visc[pick, :]

    top = lax.broadcasted_iota(jnp.int32, ext.shape[2:], 1) == ext.shape[3] - 1
    first = start[0]

    @pl.loop(0, rows)
    def _(y):
        nu = ext[3, y + 1]
        face_x = 0.5 * (nu + xroll(nu, -1))
        face_z = jnp.where(top, 0.0, 0.5 * (nu + zroll(nu, -1)))
        face_up = 0.5 * (nu + ext[3, y + 2])
        face_down = 0.5 * (nu + ext[3, y])
        for c in range(3):
            u = ext[c, y + 1]
            flux_x = face_x * (xroll(u, -1) - u)
            flux_z = face_z * (zroll(u, -1) - u)
            across_y = face_up * (ext[c, y + 2] - u) - face_down * (u - ext[c, y])
            new = u + (flux_x - xroll(flux_x, 1)) + across_y + (flux_z - zroll(flux_z, 1))
            if c == 0:
                mask = turb[pl.ds(y, nx, stride=rows), :].astype(jnp.float32)
                new = new - 0.5 * thrust_coef * mask * new * jnp.abs(new)
            out[c, y] = new
            cur = out[c, y, pl.ds(first, FR), :]
            fresh = pre[c, pl.ds(y, FR, stride=rows), :]
            out[c, y, pl.ds(first, FR), :] = cur + prof[...] * (fresh - cur)


def solve_kernel(slabs, total, b, fwd_x, fwd_z, mu, q, wrap, dhat, inc_out, vh, ssend, srecv, back, inc, hsend, hrecv, send1, recv1, send2, recv2):
    sim, me = lax.axis_index("sim"), lax.axis_index("slab")
    after, before = lax.rem(me + 1, slabs), lax.rem(me + slabs - 1, slabs)
    rows, nx, nz = dhat.shape
    share = nx // slabs
    barrier = pltpu.get_barrier_semaphore()

    @pl.loop(1, slabs)
    def _(k):
        pl.semaphore_signal(barrier, inc=1, device_id=(sim, lax.rem(me + k, slabs)), device_id_type=MESH)

    pl.semaphore_wait(barrier, slabs - 1)
    to_after = pltpu.make_async_remote_copy(b.at[1, rows - 1], vh.at[0], hsend.at[0], hrecv.at[0], device_id=(sim, after), device_id_type=MESH)
    to_before = pltpu.make_async_remote_copy(b.at[1, 0], vh.at[1], hsend.at[1], hrecv.at[1], device_id=(sim, before), device_id_type=MESH)
    to_after.start()
    to_before.start()
    lane = lax.broadcasted_iota(jnp.int32, (nx, nz), 1)

    def row(y, v_down, v_up):
        u, w = b[0, y], b[2, y]
        w_up = jnp.where(lane == nz - 1, w, zroll(w, -1))
        w_down = jnp.where(lane == 0, w, zroll(w, 1))
        d = 0.5 * (xroll(u, -1) - xroll(u, 1)) + 0.5 * (v_up - v_down) + 0.5 * (w_up - w_down)
        dhat[y] = dot(fwd_x[...], dot(d, fwd_z[...]))

    @pl.loop(1, rows - 1)
    def _(y):
        row(y, b[1, y - 1], b[1, y + 1])

    to_after.wait()
    to_before.wait()
    row(0, vh[0], b[1, 1])
    row(rows - 1, b[1, rows - 2], vh[1])

    small = (share, nz)
    at_row = lax.broadcasted_iota(jnp.int32, small, 0)
    at_lane = lax.broadcasted_iota(jnp.int32, small, 1)

    @pl.loop(0, slabs)
    def _(k):
        peer = lax.rem(me + k, slabs)
        pick = pl.ds(pl.multiple_of(peer * share, share), share)
        decay = mu[pick, :]
        f = dhat[0, pick, :]
        for y in range(1, rows):
            f = dhat[y, pick, :] + decay * f
        g = dhat[rows - 1, pick, :]
        moment = g
        for y in range(rows - 2, -1, -1):
            g = dhat[y, pick, :] + decay * g
            if y > 0:
                moment = moment + g
        zero = (at_row + peer * share + at_lane) == 0
        ssend[k, 0] = f
        ssend[k, 1] = jnp.where(zero, moment, g)

    def first(k):
        return pltpu.make_async_remote_copy(ssend.at[k], srecv.at[k], send1.at[k], recv1.at[k], device_id=(sim, lax.rem(me + k, slabs)), device_id_type=MESH)

    @pl.loop(1, slabs)
    def _(k):
        first(k).start()

    srecv[0] = ssend[0]

    @pl.loop(1, slabs)
    def _(k):
        first(k).wait()

    pick = pl.ds(pl.multiple_of(me * share, share), share)
    qq, wr = q[pick, :], wrap[pick, :]
    zero = (at_row + me * share + at_lane) == 0

    def slot(s):
        return lax.rem(me - s + slabs, slabs)

    acc_f = jnp.zeros(small, jnp.float32)
    acc_b = jnp.zeros(small, jnp.float32)
    lever = jnp.zeros(small, jnp.float32)
    for s in range(slabs):
        fl, bl = srecv[slot(s), 0], srecv[slot(s), 1]
        acc_f = fl + qq * acc_f
        lever = lever + ((rows * s) * fl + bl)
    for s in range(slabs - 1, -1, -1):
        acc_b = srecv[slot(s), 1] + qq * acc_b
    mean = acc_f * (1.0 / total)
    slope = (lever - mean * (0.5 * total * (total - 1))) * (1.0 / total)
    cur = jnp.where(zero, slope, acc_f * wr)
    for s in range(slabs):
        k = lax.rem(s - me + slabs, slabs)
        back[k, 0] = cur
        cur = srecv[slot(s), 0] + qq * cur - jnp.where(zero, mean * rows, 0.0)
    cur = acc_b * wr
    for s in range(slabs - 1, -1, -1):
        k = lax.rem(s - me + slabs, slabs)
        back[k, 1] = jnp.where(zero, mean, cur)
        cur = srecv[slot(s), 1] + qq * cur

    def second(k):
        return pltpu.make_async_remote_copy(back.at[k], inc.at[k], send2.at[k], recv2.at[k], device_id=(sim, lax.rem(me + k, slabs)), device_id_type=MESH)

    @pl.loop(1, slabs)
    def _(k):
        second(k).start()

    inc[0] = back[0]

    @pl.loop(1, slabs)
    def _(k):
        second(k).wait()

    @pl.loop(0, slabs)
    def _(k):
        owner = lax.rem(me - k + slabs, slabs)
        inc_out[owner] = inc[k]


def finish_kernel(b, dhat, inc, mu, coef, inv_x, inv_z, out, ph):
    rows, nx, nz = dhat.shape
    slabs, _, share, _ = inc.shape

    @pl.loop(0, slabs)
    def _(p):
        pick = pl.ds(pl.multiple_of(p * share, share), share)
        decay, scale = mu[pick, :], coef[pick, :]
        f_in, b_in = inc[p, 0], inc[p, 1]
        f = f_in
        for y in range(rows):
            f = dhat[y, pick, :] + decay * f
            ph[y + 1, pick, :] = f
        ph[rows + 1, pick, :] = scale * (b_in + decay * f)
        g = b_in
        for y in range(rows - 1, -1, -1):
            d = dhat[y, pick, :]
            g = d + decay * g
            ph[y + 1, pick, :] = scale * (ph[y + 1, pick, :] + g - d)
        ph[0, pick, :] = scale * (f_in + decay * g)

    tile = (8, nz)
    zero = (lax.broadcasted_iota(jnp.int32, tile, 0) + lax.broadcasted_iota(jnp.int32, tile, 1)) == 0
    slope, mean = inc[0, 0, :8, :], inc[0, 1, :8, :]
    level = jnp.zeros(tile, jnp.float32)
    for y in range(rows + 2):
        ph[y, :8, :] = jnp.where(zero, level, ph[y, :8, :])
        level = level + slope
        if y < rows:
            slope = slope + (dhat[y, :8, :] - mean)

    @pl.loop(0, rows + 2)
    def _(y):
        ph[y] = dot(inv_x[...], dot(ph[y], inv_z[...]))

    lane = lax.broadcasted_iota(jnp.int32, (nx, nz), 1)

    @pl.loop(0, rows)
    def _(y):
        p = ph[y + 1]
        pick = pl.ds(y, nx, stride=rows)
        out[0, pick, :] = b[0, y] - 0.5 * (xroll(p, -1) - xroll(p, 1))
        out[1, pick, :] = b[1, y] - 0.5 * (ph[y + 2] - ph[y])
        p_up = jnp.where(lane == nz - 1, p, zroll(p, -1))
        p_down = jnp.where(lane == 0, p, zroll(p, 1))
        out[2, pick, :] = b[2, y] - 0.5 * (p_up - p_down)


def local(velocity, viscosity, turbines, fringe_start):
    import functools as ft

    sims, slabs = lax.axis_size("sim"), lax.axis_size("slab")
    _, _, nx, rows, nz = velocity.shape
    total = rows * slabs
    share = nx // slabs
    f32 = jnp.float32
    sds = lambda *s: jax.ShapeDtypeStruct(s, f32)
    vel = velocity.reshape(3, nx * rows, nz)
    visc = viscosity.reshape(nx * rows, nz)
    turb = turbines.reshape(nx * rows, nz)
    table = tables(nx, total, nz, rows)
    params = lambda **k: pltpu.CompilerParams(vmem_limit_bytes=GRANT, **k)

    fringe = lax.dynamic_slice_in_dim(velocity[0], fringe_start[0], FR, 1).reshape(3, FR * rows, nz)
    lo, hi = pl.pallas_call(
        ft.partial(edges_kernel, rows),
        out_shape=(sds(4, nx, nz), sds(4, nx, nz)),
        in_specs=[full()] * 2,
        out_specs=(full(), full()),
        compiler_params=params(),
        name="edges",
    )(vel, visc)
    DMA = pltpu.SemaphoreType.DMA
    left, right, pre = pl.pallas_call(
        ft.partial(halo_kernel, sims, slabs),
        out_shape=(sds(4, nx, nz), sds(4, nx, nz), sds(3, FR * rows, nz)),
        in_specs=[full()] * 3,
        out_specs=(full(),) * 3,
        scratch_shapes=[DMA((2,)), DMA((2,)), DMA((max(sims - 1, 1),)), DMA],
        compiler_params=params(collective_id=0, has_side_effects=True),
        name="halo",
    )(lo, hi, fringe)
    active = (lax.axis_index("sim") != 0).astype(f32)
    profile = np.sin(math.pi * (np.arange(FR) + 0.5) / FR) ** 2
    prof = jnp.asarray(np.repeat(profile[:, None], nz, 1), f32) * active
    blended = pl.pallas_call(
        ft.partial(step_kernel, rows),
        out_shape=sds(3, rows, nx, nz),
        in_specs=[full(pltpu.SMEM)] + [full()] * 7,
        out_specs=full(),
        scratch_shapes=[VM((4, rows + 2, nx, nz), f32)],
        compiler_params=params(),
        name="step",
    )(fringe_start, vel, visc, turb, left, right, pre, prof)
    pair = (slabs, 2, share, nz)
    dhat, inc = pl.pallas_call(
        ft.partial(solve_kernel, slabs, total),
        out_shape=(sds(rows, nx, nz), sds(*pair)),
        in_specs=[full()] * 6,
        out_specs=(full(), full()),
        scratch_shapes=[VM((2, nx, nz), f32)] + [VM(pair, f32)] * 4 + [DMA((2,)), DMA((2,))] + [DMA((slabs,))] * 4,
        compiler_params=params(collective_id=1, has_side_effects=True),
        name="solve",
    )(blended, table["fwd_x"], table["fwd_z"], table["mu"], table["q"], table["wrap"])
    out = pl.pallas_call(
        finish_kernel,
        out_shape=sds(3, nx * rows, nz),
        in_specs=[full()] * 7,
        out_specs=full(),
        scratch_shapes=[VM((rows + 2, nx, nz), f32)],
        compiler_params=params(),
        name="finish",
    )(blended, dhat, inc, table["mu"], table["coef"], table["inv_x"], table["inv_z"])
    return out.reshape(1, 3, nx, rows, nz)


def solution(mesh):
    return jax.shard_map(
        local,
        mesh=mesh,
        in_specs=(
            P("sim", None, None, "slab", None),
            P("sim", None, "slab", None),
            P("sim", None, "slab", None),
            P(),
        ),
        out_specs=P("sim", None, None, "slab", None),
        check_vma=False,
    )
```

```python
import functools
import math

import jax
import jax.numpy as jnp
import numpy as np
from jax import lax
from jax.experimental import pallas as pl
from jax.experimental.pallas import tpu as pltpu
from jax.sharding import PartitionSpec as P

FR = 32

thrust_coef = 0.75
MESH = pl.DeviceIdType.MESH
VM = pltpu.VMEM
GRANT = 60 * 1024 * 1024


def split(value):
    high = value.astype(jnp.bfloat16)
    return high, (value - high.astype(jnp.float32)).astype(jnp.bfloat16)


def split_table(table, axis):
    high = table.astype(jnp.bfloat16)
    low = (table - high.astype(np.float32)).astype(jnp.bfloat16)
    return np.concatenate([high, high, low], axis)


def dot(a, b):
    return jnp.dot(a, b, preferred_element_type=jnp.float32)


def parts(value):
    high, rest = split(value)
    mid = value - high.astype(jnp.float32)
    low = mid - rest.astype(jnp.float32)
    return jnp.concatenate([high, rest, low.astype(jnp.bfloat16)], 0)


def along_z(value, table):
    high, low = split(value)
    return dot(jnp.concatenate([high, low, high], 1), table)


def along_x(table, value):
    high, low = split(value)
    return dot(table, jnp.concatenate([high, low, high], 0))


def transform(table_x, pair, table_z):
    nx, nz = pair[0].shape
    mid = along_z(jnp.concatenate(pair, 0), table_z)
    both = along_x(table_x, jnp.concatenate([mid[:nx], mid[nx:]], 1))
    return both[:, :nz], both[:, nz:]


def full(space=VM):
    return pl.BlockSpec(memory_space=space)


def tables(nx, ny, nz, rows):
    half = nx // 2
    wave = np.concatenate([np.arange(half), [half], np.arange(1, half)])
    at = np.arange(nx)
    angle = 2.0 * np.pi * ((wave[:, None] * at[None, :]) % nx) / nx
    is_sine = (np.arange(nx) > half)[:, None]
    fwd_x = np.where(is_sine, -np.sin(angle), np.cos(angle))
    weight = np.where((wave == 0) | (wave == half), 1.0, 2.0) / nx
    inv_x = (fwd_x * weight[:, None]).T
    m = np.arange(nz)
    cos_z = np.cos(np.pi * ((m[:, None] * (2 * m[None, :] + 1)) % (4 * nz)) / (2.0 * nz))
    inv_z = cos_z * (np.where(m == 0, 1.0, 2.0) / nz)[:, None]
    a = (4.0 * np.sin(np.pi * wave / nx) ** 2)[:, None] + (4.0 * np.sin(np.pi * m / (2.0 * nz)) ** 2)[None, :]
    root = np.sqrt(a + a * a / 4.0)
    mu = 1.0 / (1.0 + a / 2.0 + root)
    zero = a == 0.0
    coef = np.where(zero, 0.0, -1.0 / np.where(zero, 1.0, 2.0 * root))
    q = mu**rows
    wrap = 1.0 / np.where(zero, 1.0, 1.0 - mu**ny)
    f32 = lambda t: np.asarray(t, np.float32)
    return dict(fwd_x=split_table(f32(fwd_x), 1), inv_x=split_table(f32(inv_x), 1), fwd_z=split_table(f32(cos_z.T), 0), inv_z=split_table(f32(inv_z), 0), mu=f32(mu), coef=f32(coef), q=f32(q), wrap=f32(wrap))


def xroll(value, shift):
    return pltpu.roll(value, shift % value.shape[0], 0)


def zroll(value, shift):
    return pltpu.roll(value, shift % value.shape[1], 1)


def main_kernel(sims, slabs, start, vel_hbm, visc_hbm, turb_hbm, fringe, prof, fwd_x, fwd_z, mu, coef, q, wrap, inv_x, inv_z, bl_out, p_out,
                vel, visc, turb, edge, halo, pre, place, wfull, ext, bl, dhat, ph, pbuf, vh, ssend, srecv, back, inc,
                load, store, send, recv, psend, precv, hsend, hrecv, send1, recv1, send2, recv2):
    sim, me = lax.axis_index("sim"), lax.axis_index("slab")
    after, before = lax.rem(me + 1, slabs), lax.rem(me + slabs - 1, slabs)
    rows, nx, nz = dhat.shape
    total = rows * slabs
    share = nx // slabs
    loads = [pltpu.make_async_copy(a, b, load.at[i]) for i, (a, b) in enumerate(((vel_hbm, vel), (visc_hbm, visc), (turb_hbm, turb)))]
    for copy in loads:
        copy.start()
    barrier = pltpu.get_barrier_semaphore()

    @pl.loop(1, slabs)
    def _(k):
        pl.semaphore_signal(barrier, inc=1, device_id=(sim, lax.rem(me + k, slabs)), device_id_type=MESH)

    @pl.when(sim == 0)
    def _():
        for other in range(1, sims):
            pl.semaphore_signal(barrier, inc=1, device_id=(other, me), device_id_type=MESH)

    @pl.when(sim != 0)
    def _():
        pl.semaphore_signal(barrier, inc=1, device_id=(0, me), device_id_type=MESH)

    first = start[0]
    loads[0].wait()
    loads[1].wait()
    for c in range(4):
        for side, at in ((0, 0), (1, rows - 1)):
            pick = pl.ds(at, nx, stride=rows)
            edge[side, c] = visc[pick, :] if c == 3 else vel[c, pick, :]

    @pl.when(sim == 0)
    def _():
        pl.semaphore_wait(barrier, slabs - 1 + sims - 1)

    @pl.when(sim != 0)
    def _():
        pl.semaphore_wait(barrier, slabs)

    to_after = pltpu.make_async_remote_copy(edge.at[1], halo.at[0], send.at[0], recv.at[0], device_id=(sim, after), device_id_type=MESH)
    to_before = pltpu.make_async_remote_copy(edge.at[0], halo.at[1], send.at[1], recv.at[1], device_id=(sim, before), device_id_type=MESH)
    to_after.start()
    to_before.start()

    def give(other):
        return pltpu.make_async_remote_copy(fringe, pre, psend.at[other - 1], precv, device_id=(other, me), device_id_type=MESH)

    @pl.when(sim == 0)
    def _():
        for other in range(1, sims):
            give(other).start()

    @pl.loop(0, rows)
    def _(y):
        pick = pl.ds(y, nx, stride=rows)
        for c in range(3):
            ext[c, y + 1] = vel[c, pick, :]
        ext[3, y + 1] = visc[pick, :]

    lane = lax.broadcasted_iota(jnp.int32, (nx, nz), 1)
    part = lax.broadcasted_iota(jnp.int32, place.shape, 1)
    row_of = lax.broadcasted_iota(jnp.int32, place.shape, 0) - first
    place[...] = (lax.rem(part, FR) == row_of).astype(jnp.float32).astype(jnp.bfloat16)
    wfull[...] = dot(place[...], parts(prof[...])) * (sim != 0).astype(jnp.float32)

    @pl.when(sim == 0)
    def _():
        pre[...] = jnp.zeros_like(pre)

    loads[2].wait()

    def diffuse(y):
        nu = ext[3, y + 1]
        face_x = 0.5 * (nu + xroll(nu, -1))
        face_z = jnp.where(lane == nz - 1, 0.0, 0.5 * (nu + zroll(nu, -1)))
        face_up = 0.5 * (nu + ext[3, y + 2])
        face_down = 0.5 * (nu + ext[3, y])
        for c in range(3):
            u = ext[c, y + 1]
            flux_x = face_x * (xroll(u, -1) - u)
            flux_z = face_z * (zroll(u, -1) - u)
            across_y = face_up * (ext[c, y + 2] - u) - face_down * (u - ext[c, y])
            new = u + (flux_x - xroll(flux_x, 1)) + across_y + (flux_z - zroll(flux_z, 1))
            if c == 0:
                mask = turb[pl.ds(y, nx, stride=rows), :].astype(jnp.float32)
                new = new - 0.5 * thrust_coef * mask * new * jnp.abs(new)
            bl[c, y] = new

    @pl.loop(1, rows - 1)
    def _(y):
        diffuse(y)

    to_after.wait()
    to_before.wait()
    for c in range(4):
        ext[c, 0] = halo[0, c]
        ext[c, rows + 1] = halo[1, c]

    @pl.loop(0, 2)
    def _(end):
        diffuse(end * (rows - 1))

    @pl.when(sim == 0)
    def _():
        for other in range(1, sims):
            give(other).wait_send()

    @pl.when(sim != 0)
    def _():
        give(1).wait_recv()

    @pl.loop(0, rows)
    def _(k):
        y = lax.rem(k + rows - 1, rows)
        rows_in = jnp.concatenate([pre[c, pl.ds(y, FR, stride=rows), :] for c in range(3)], 1)
        placed = dot(place[...], parts(rows_in))
        for c in range(3):
            cur = bl[c, y]
            bl[c, y] = cur + wfull[...] * (placed[:, c * nz : (c + 1) * nz] - cur)

    v_after = pltpu.make_async_remote_copy(bl.at[1, rows - 1], vh.at[0], hsend.at[0], hrecv.at[0], device_id=(sim, after), device_id_type=MESH)
    v_before = pltpu.make_async_remote_copy(bl.at[1, 0], vh.at[1], hsend.at[1], hrecv.at[1], device_id=(sim, before), device_id_type=MESH)
    v_after.start()
    v_before.start()
    out_copy = pltpu.make_async_copy(bl, bl_out, store.at[0])
    out_copy.start()

    def div(y, v_down, v_up):
        u, w = bl[0, y], bl[2, y]
        w_up = jnp.where(lane == nz - 1, w, zroll(w, -1))
        w_down = jnp.where(lane == 0, w, zroll(w, 1))
        return 0.5 * (xroll(u, -1) - xroll(u, 1)) + 0.5 * (v_up - v_down) + 0.5 * (w_up - w_down)

    @pl.loop(0, rows // 2 - 1)
    def _(k):
        y = 2 * k + 1
        pair = [div(y + i, bl[1, y + i - 1], bl[1, y + i + 1]) for i in range(2)]
        dhat[y], dhat[y + 1] = transform(fwd_x[...], pair, fwd_z[...])

    v_after.wait()
    v_before.wait()
    pair = [div(0, vh[0], bl[1, 1]), div(rows - 1, bl[1, rows - 2], vh[1])]
    dhat[0], dhat[rows - 1] = transform(fwd_x[...], pair, fwd_z[...])

    small = (share, nz)
    at_row = lax.broadcasted_iota(jnp.int32, small, 0)
    at_lane = lax.broadcasted_iota(jnp.int32, small, 1)

    @pl.loop(0, slabs)
    def _(k):
        peer = lax.rem(me + k, slabs)
        pick = pl.ds(pl.multiple_of(peer * share, share), share)
        decay = mu[pick, :]
        f = dhat[0, pick, :]
        for y in range(1, rows):
            f = dhat[y, pick, :] + decay * f
        g = dhat[rows - 1, pick, :]
        moment = g
        for y in range(rows - 2, -1, -1):
            g = dhat[y, pick, :] + decay * g
            if y > 0:
                moment = moment + g
        zero = (at_row + peer * share + at_lane) == 0
        ssend[k, 0] = f
        ssend[k, 1] = jnp.where(zero, moment, g)

    def first(k):
        return pltpu.make_async_remote_copy(ssend.at[k], srecv.at[k], send1.at[k], recv1.at[k], device_id=(sim, lax.rem(me + k, slabs)), device_id_type=MESH)

    @pl.loop(1, slabs)
    def _(k):
        first(k).start()

    srecv[0] = ssend[0]

    @pl.loop(1, slabs)
    def _(k):
        first(k).wait()

    pick = pl.ds(pl.multiple_of(me * share, share), share)
    qq, wr = q[pick, :], wrap[pick, :]
    zero = (at_row + me * share + at_lane) == 0

    def slot(s):
        return lax.rem(me - s + slabs, slabs)

    acc_f = jnp.zeros(small, jnp.float32)
    acc_b = jnp.zeros(small, jnp.float32)
    lever = jnp.zeros(small, jnp.float32)
    for s in range(slabs):
        fl, bl = srecv[slot(s), 0], srecv[slot(s), 1]
        acc_f = fl + qq * acc_f
        lever = lever + ((rows * s) * fl + bl)
    for s in range(slabs - 1, -1, -1):
        acc_b = srecv[slot(s), 1] + qq * acc_b
    mean = acc_f * (1.0 / total)
    slope = (lever - mean * (0.5 * total * (total - 1))) * (1.0 / total)
    cur = jnp.where(zero, slope, acc_f * wr)
    for s in range(slabs):
        k = lax.rem(s - me + slabs, slabs)
        back[k, 0] = cur
        cur = srecv[slot(s), 0] + qq * cur - jnp.where(zero, mean * rows, 0.0)
    cur = acc_b * wr
    for s in range(slabs - 1, -1, -1):
        k = lax.rem(s - me + slabs, slabs)
        back[k, 1] = jnp.where(zero, mean, cur)
        cur = srecv[slot(s), 1] + qq * cur

    def second(k):
        return pltpu.make_async_remote_copy(back.at[k], inc.at[k], send2.at[k], recv2.at[k], device_id=(sim, lax.rem(me + k, slabs)), device_id_type=MESH)

    @pl.loop(1, slabs)
    def _(k):
        second(k).start()

    inc[0] = back[0]

    @pl.loop(1, slabs)
    def _(k):
        second(k).wait()

    @pl.loop(0, slabs)
    def _(k):
        p = lax.rem(me - k + slabs, slabs)
        pick = pl.ds(pl.multiple_of(p * share, share), share)
        decay, scale = mu[pick, :], coef[pick, :]
        f_in, b_in = inc[k, 0], inc[k, 1]
        f = f_in
        for y in range(rows):
            f = dhat[y, pick, :] + decay * f
            ph[y + 1, pick, :] = f
        ph[rows + 1, pick, :] = scale * (b_in + decay * f)
        g = b_in
        for y in range(rows - 1, -1, -1):
            d = dhat[y, pick, :]
            g = d + decay * g
            ph[y + 1, pick, :] = scale * (ph[y + 1, pick, :] + g - d)
        ph[0, pick, :] = scale * (f_in + decay * g)

    tile = (8, nz)
    zero = (lax.broadcasted_iota(jnp.int32, tile, 0) + lax.broadcasted_iota(jnp.int32, tile, 1)) == 0
    slope, mean = inc[me, 0, :8, :], inc[me, 1, :8, :]
    level = jnp.zeros(tile, jnp.float32)
    for y in range(rows + 2):
        ph[y, :8, :] = jnp.where(zero, level, ph[y, :8, :])
        level = level + slope
        if y < rows:
            slope = slope + (dhat[y, :8, :] - mean)

    @pl.loop(0, rows // 2 + 1)
    def _(k):
        a, b = transform(inv_x[...], [ph[2 * k], ph[2 * k + 1]], inv_z[...])
        for i, p in ((0, a), (1, b)):
            y = 2 * k + i
            pbuf[y, pl.ds(8, nx), :] = p
            pbuf[y, pl.ds(0, 8), :] = p[nx - 8 :]
            pbuf[y, pl.ds(nx + 8, 8), :] = p[:8]

    p_copy = pltpu.make_async_copy(pbuf, p_out, store.at[1])
    p_copy.start()
    out_copy.wait()
    p_copy.wait()


def gradient_kernel(b, p, out):
    _, rows, chunk, nz = b.shape
    base = pl.multiple_of(pl.program_id(0) * chunk, chunk)
    lane = lax.broadcasted_iota(jnp.int32, (chunk, nz), 1)

    @pl.loop(0, rows)
    def _(y):
        here = p[y + 1, pl.ds(base + 8, chunk), :]
        pick = pl.ds(y, chunk, stride=rows)
        out[0, pick, :] = b[0, y] - 0.5 * (p[y + 1, pl.ds(base + 9, chunk), :] - p[y + 1, pl.ds(base + 7, chunk), :])
        out[1, pick, :] = b[1, y] - 0.5 * (p[y + 2, pl.ds(base + 8, chunk), :] - p[y, pl.ds(base + 8, chunk), :])
        p_up = jnp.where(lane == nz - 1, here, zroll(here, -1))
        p_down = jnp.where(lane == 0, here, zroll(here, 1))
        out[2, pick, :] = b[2, y] - 0.5 * (p_up - p_down)


def local(velocity, viscosity, turbines, fringe_start):
    sims, slabs = lax.axis_size("sim"), lax.axis_size("slab")
    _, _, nx, rows, nz = velocity.shape
    total = rows * slabs
    share = nx // slabs
    f32 = jnp.float32
    sds = lambda *s: jax.ShapeDtypeStruct(s, f32)
    vel = velocity.reshape(3, nx * rows, nz)
    visc = viscosity.reshape(nx * rows, nz)
    turb = turbines.reshape(nx * rows, nz)
    fringe = lax.dynamic_slice_in_dim(velocity[0], fringe_start[0], FR, 1).reshape(3, FR * rows, nz)
    t = tables(nx, total, nz, rows)
    profile = np.sin(math.pi * (np.arange(FR) + 0.5) / FR) ** 2
    prof = np.repeat(profile[:, None], nz, 1).astype(np.float32)
    DMA = pltpu.SemaphoreType.DMA
    buf = lambda *s: VM(s, f32)
    pair = (slabs, 2, share, nz)
    scratch = [
        buf(3, nx * rows, nz), buf(nx * rows, nz), VM((nx * rows, nz), jnp.int32), buf(2, 4, nx, nz), buf(2, 4, nx, nz),
        buf(3, FR * rows, nz), VM((nx, 3 * FR), jnp.bfloat16), buf(nx, nz), buf(4, rows + 2, nx, nz),
        buf(3, rows, nx, nz), buf(rows, nx, nz), buf(rows + 2, nx, nz), buf(rows + 2, nx + 16, nz), buf(2, nx, nz),
        buf(*pair), buf(*pair), buf(*pair), buf(*pair),
        DMA((3,)), DMA((2,)), DMA((2,)), DMA((2,)), DMA((max(sims - 1, 1),)), DMA, DMA((2,)), DMA((2,)),
    ] + [DMA((slabs,))] * 4
    blended, pressure = pl.pallas_call(
        functools.partial(main_kernel, sims, slabs),
        out_shape=(sds(3, rows, nx, nz), sds(rows + 2, nx + 16, nz)),
        in_specs=[full(pltpu.SMEM)] + [full(pl.ANY)] * 4 + [full()] * 9,
        out_specs=(full(pl.ANY), full(pl.ANY)),
        scratch_shapes=scratch,
        compiler_params=pltpu.CompilerParams(vmem_limit_bytes=GRANT, collective_id=0, has_side_effects=True),
        name="main",
    )(fringe_start, vel, visc, turb, fringe, prof, t["fwd_x"], t["fwd_z"], t["mu"], t["coef"], t["q"], t["wrap"], t["inv_x"], t["inv_z"])
    chunk = nx // 8
    out = pl.pallas_call(
        gradient_kernel,
        out_shape=sds(3, nx * rows, nz),
        grid=(nx // chunk,),
        in_specs=[
            pl.BlockSpec((3, rows, chunk, nz), lambda i: (0, 0, i, 0)),
            pl.BlockSpec((rows + 2, nx + 16, nz), lambda i: (0, 0, 0)),
        ],
        out_specs=pl.BlockSpec((3, chunk * rows, nz), lambda i: (0, i, 0)),
        compiler_params=pltpu.CompilerParams(vmem_limit_bytes=GRANT),
        name="gradient",
    )(blended, pressure)
    return out.reshape(1, 3, nx, rows, nz)


def solution(mesh):
    return jax.shard_map(
        local,
        mesh=mesh,
        in_specs=(
            P("sim", None, None, "slab", None),
            P("sim", None, "slab", None),
            P("sim", None, "slab", None),
            P(),
        ),
        out_specs=P("sim", None, None, "slab", None),
        check_vma=False,
    )
```

```python
import functools
import math

import jax
import jax.numpy as jnp
import numpy as np
from jax import lax
from jax.experimental import pallas as pl
from jax.experimental.pallas import tpu as pltpu
from jax.sharding import PartitionSpec as P

FR = 32

thrust_coef = 0.75
MESH = pl.DeviceIdType.MESH
VM = pltpu.VMEM
GRANT = 60 * 1024 * 1024


def split(value):
    high = value.astype(jnp.bfloat16)
    return high, (value - high.astype(jnp.float32)).astype(jnp.bfloat16)


def split_table(table, axis):
    high = table.astype(jnp.bfloat16)
    low = (table - high.astype(np.float32)).astype(jnp.bfloat16)
    return np.concatenate([high, high, low], axis)


def dot(a, b):
    return jnp.dot(a, b, preferred_element_type=jnp.float32)


def parts(value):
    high, rest = split(value)
    mid = value - high.astype(jnp.float32)
    low = mid - rest.astype(jnp.float32)
    return jnp.concatenate([high, rest, low.astype(jnp.bfloat16)], 0)


def along_z(value, table):
    high, low = split(value)
    return dot(jnp.concatenate([high, low, high], 1), table)


def along_x(table, value):
    high, low = split(value)
    return dot(table, jnp.concatenate([high, low, high], 0))


def transform(table_x, pair, table_z):
    nx, nz = pair[0].shape
    mid = along_z(jnp.concatenate(pair, 0), table_z)
    both = along_x(table_x, jnp.concatenate([mid[:nx], mid[nx:]], 1))
    return both[:, :nz], both[:, nz:]


def full(space=VM):
    return pl.BlockSpec(memory_space=space)


def tables(nx, ny, nz, rows):
    half = nx // 2
    wave = np.concatenate([np.arange(half), [half], np.arange(1, half)])
    at = np.arange(nx)
    angle = 2.0 * np.pi * ((wave[:, None] * at[None, :]) % nx) / nx
    is_sine = (np.arange(nx) > half)[:, None]
    fwd_x = np.where(is_sine, -np.sin(angle), np.cos(angle))
    weight = np.where((wave == 0) | (wave == half), 1.0, 2.0) / nx
    inv_x = (fwd_x * weight[:, None]).T
    m = np.arange(nz)
    cos_z = np.cos(np.pi * ((m[:, None] * (2 * m[None, :] + 1)) % (4 * nz)) / (2.0 * nz))
    inv_z = cos_z * (np.where(m == 0, 1.0, 2.0) / nz)[:, None]
    a = (4.0 * np.sin(np.pi * wave / nx) ** 2)[:, None] + (4.0 * np.sin(np.pi * m / (2.0 * nz)) ** 2)[None, :]
    root = np.sqrt(a + a * a / 4.0)
    mu = 1.0 / (1.0 + a / 2.0 + root)
    zero = a == 0.0
    coef = np.where(zero, 0.0, -1.0 / np.where(zero, 1.0, 2.0 * root))
    q = mu**rows
    wrap = 1.0 / np.where(zero, 1.0, 1.0 - mu**ny)
    f32 = lambda t: np.asarray(t, np.float32)
    return dict(fwd_x=split_table(f32(fwd_x), 1), inv_x=split_table(f32(inv_x), 1), fwd_z=split_table(f32(cos_z.T), 0), inv_z=split_table(f32(inv_z), 0), mu=f32(mu), coef=f32(coef), q=f32(q), wrap=f32(wrap))


def xroll(value, shift):
    return pltpu.roll(value, shift % value.shape[0], 0)


def zroll(value, shift):
    return pltpu.roll(value, shift % value.shape[1], 1)


def main_kernel(sims, slabs, start, vel_hbm, visc_hbm, turb_hbm, fringe, prof, fwd_x, fwd_z, mu, coef, q, wrap, inv_x, inv_z, bl_out, p_out,
                vel, visc, turb, edge, halo, pre, place, wfull, ext, bl, dhat, ph, pbuf, vh, ve, vf, pv, ssend, srecv, back, inc,
                load, store, send, recv, psend, precv, hsend, hrecv, send1, recv1, send2, recv2):
    sim, me = lax.axis_index("sim"), lax.axis_index("slab")
    after, before = lax.rem(me + 1, slabs), lax.rem(me + slabs - 1, slabs)
    rows, nx, nz = dhat.shape
    total = rows * slabs
    share = nx // slabs
    loads = [pltpu.make_async_copy(a, b, load.at[i]) for i, (a, b) in enumerate(((vel_hbm, vel), (visc_hbm, visc), (turb_hbm, turb)))]
    for copy in loads:
        copy.start()
    barrier = pltpu.get_barrier_semaphore()

    @pl.loop(1, slabs)
    def _(k):
        pl.semaphore_signal(barrier, inc=1, device_id=(sim, lax.rem(me + k, slabs)), device_id_type=MESH)

    @pl.when(sim == 0)
    def _():
        for other in range(1, sims):
            for peer in (me, after, before):
                pl.semaphore_signal(barrier, inc=1, device_id=(other, peer), device_id_type=MESH)

    @pl.when(sim != 0)
    def _():
        for peer in (me, after, before):
            pl.semaphore_signal(barrier, inc=1, device_id=(0, peer), device_id_type=MESH)

    @pl.when(sim == 0)
    def _():
        pl.semaphore_wait(barrier, slabs - 1 + 3 * (sims - 1))

    @pl.when(sim != 0)
    def _():
        pl.semaphore_wait(barrier, slabs - 1 + 3)

    chunks = fringe.shape[0]

    def give(other, j):
        return pltpu.make_async_remote_copy(fringe.at[j], pre.at[j], psend.at[other - 1, j], precv.at[j], device_id=(other, me), device_id_type=MESH)

    def give_edge(other, side):
        peer = before if side == 0 else after
        return pltpu.make_async_remote_copy(vf.at[side], pv.at[1 - side], psend.at[other - 1, chunks + side], precv.at[chunks + 1 - side], device_id=(other, peer), device_id_type=MESH)

    @pl.when(sim == 0)
    def _():
        for other in range(1, sims):
            give(other, 0).start()

    first = start[0]
    loads[0].wait()
    loads[1].wait()
    for c in range(4):
        for side, at in ((0, 0), (1, rows - 1)):
            pick = pl.ds(at, nx, stride=rows)
            edge[side, c] = visc[pick, :] if c == 3 else vel[c, pick, :]

    to_after = pltpu.make_async_remote_copy(edge.at[1], halo.at[0], send.at[0], recv.at[0], device_id=(sim, after), device_id_type=MESH)
    to_before = pltpu.make_async_remote_copy(edge.at[0], halo.at[1], send.at[1], recv.at[1], device_id=(sim, before), device_id_type=MESH)
    to_after.start()
    to_before.start()

    @pl.when(sim == 0)
    def _():
        col = lax.rem(lax.broadcasted_iota(jnp.int32, (FR, 3 * nx), 1), nx)
        at = lax.broadcasted_iota(jnp.int32, (FR, 3 * nx), 0) + first
        take = (col == at).astype(jnp.float32).astype(jnp.bfloat16)
        for side in range(2):
            vf[side] = dot(take, parts(edge[side, 1]))
            pv[side] = jnp.zeros_like(pv[side])
        for other in range(1, sims):
            for side in range(2):
                give_edge(other, side).start()
            for j in range(1, chunks):
                give(other, j).start()

    @pl.loop(0, rows)
    def _(y):
        pick = pl.ds(y, nx, stride=rows)
        for c in range(3):
            ext[c, y + 1] = vel[c, pick, :]
        ext[3, y + 1] = visc[pick, :]

    lane = lax.broadcasted_iota(jnp.int32, (nx, nz), 1)
    part = lax.broadcasted_iota(jnp.int32, place.shape, 1)
    row_of = lax.broadcasted_iota(jnp.int32, place.shape, 0) - first
    place[...] = (lax.rem(part, FR) == row_of).astype(jnp.float32).astype(jnp.bfloat16)
    wfull[...] = dot(place[...], parts(prof[...])) * (sim != 0).astype(jnp.float32)

    @pl.when(sim == 0)
    def _():
        pre[...] = jnp.zeros_like(pre)

    loads[2].wait()

    def diffuse(y):
        nu = ext[3, y + 1]
        face_x = 0.5 * (nu + xroll(nu, -1))
        face_z = jnp.where(lane == nz - 1, 0.0, 0.5 * (nu + zroll(nu, -1)))
        face_up = 0.5 * (nu + ext[3, y + 2])
        face_down = 0.5 * (nu + ext[3, y])
        for c in range(3):
            u = ext[c, y + 1]
            flux_x = face_x * (xroll(u, -1) - u)
            flux_z = face_z * (zroll(u, -1) - u)
            across_y = face_up * (ext[c, y + 2] - u) - face_down * (u - ext[c, y])
            new = u + (flux_x - xroll(flux_x, 1)) + across_y + (flux_z - zroll(flux_z, 1))
            if c == 0:
                mask = turb[pl.ds(y, nx, stride=rows), :].astype(jnp.float32)
                new = new - 0.5 * thrust_coef * mask * new * jnp.abs(new)
            bl[c, y] = new

    @pl.loop(1, rows - 1)
    def _(y):
        diffuse(y)

    to_after.wait()
    to_before.wait()
    for c in range(4):
        ext[c, 0] = halo[0, c]
        ext[c, rows + 1] = halo[1, c]

    @pl.loop(0, 2)
    def _(end):
        diffuse(end * (rows - 1))

    ve[0] = bl[1, 0]
    ve[1] = bl[1, rows - 1]

    def blend(cur, placed):
        return cur + wfull[...] * (placed - cur)

    def div(y, v_down, v_up):
        u, w = bl[0, y], bl[2, y]
        w_up = jnp.where(lane == nz - 1, w, zroll(w, -1))
        w_down = jnp.where(lane == 0, w, zroll(w, 1))
        return 0.5 * (xroll(u, -1) - xroll(u, 1)) + 0.5 * (v_up - v_down) + 0.5 * (w_up - w_down)

    v_after = pltpu.make_async_remote_copy(ve.at[1], vh.at[0], hsend.at[0], hrecv.at[0], device_id=(sim, after), device_id_type=MESH)
    v_before = pltpu.make_async_remote_copy(ve.at[0], vh.at[1], hsend.at[1], hrecv.at[1], device_id=(sim, before), device_id_type=MESH)
    part_rows = rows // chunks
    for j in range(chunks):

        @pl.when(sim != 0)
        def _():
            give(1, j).wait_recv()

        if j == 0:
            v_after.start()
            v_before.start()

        @pl.loop(0, part_rows)
        def _(i):
            y = j * part_rows + i
            rows_in = jnp.concatenate([pre[j, c, pl.ds(i, FR, stride=part_rows), :] for c in range(3)], 1)
            placed = dot(place[...], parts(rows_in))
            for c in range(3):
                bl[c, y] = blend(bl[c, y], placed[:, c * nz : (c + 1) * nz])

        @pl.loop(max(0, (part_rows // 2) * j - 1), (part_rows // 2) * (j + 1) - 1)
        def _(k):
            y = 2 * k + 1
            pair = [div(y + i, bl[1, y + i - 1], bl[1, y + i + 1]) for i in range(2)]
            dhat[y], dhat[y + 1] = transform(fwd_x[...], pair, fwd_z[...])

    out_copy = pltpu.make_async_copy(bl, bl_out, store.at[0])
    out_copy.start()
    v_after.wait()
    v_before.wait()

    @pl.when(sim != 0)
    def _():
        for side in range(2):
            give_edge(1, side).wait_recv()

    @pl.when(sim == 0)
    def _():
        for other in range(1, sims):
            for j in range(chunks):
                give(other, j).wait_send()
            for side in range(2):
                give_edge(other, side).wait_send()

    edge_rows = dot(place[...], parts(jnp.concatenate([pv[0], pv[1]], 1)))
    for side in range(2):
        vh[side] = blend(vh[side], edge_rows[:, side * nz : (side + 1) * nz])
    pair = [div(0, vh[0], bl[1, 1]), div(rows - 1, bl[1, rows - 2], vh[1])]
    dhat[0], dhat[rows - 1] = transform(fwd_x[...], pair, fwd_z[...])

    small = (share, nz)
    at_row = lax.broadcasted_iota(jnp.int32, small, 0)
    at_lane = lax.broadcasted_iota(jnp.int32, small, 1)

    @pl.loop(0, slabs)
    def _(k):
        peer = lax.rem(me + k, slabs)
        pick = pl.ds(pl.multiple_of(peer * share, share), share)
        decay = mu[pick, :]
        f = dhat[0, pick, :]
        for y in range(1, rows):
            f = dhat[y, pick, :] + decay * f
        g = dhat[rows - 1, pick, :]
        moment = g
        for y in range(rows - 2, -1, -1):
            g = dhat[y, pick, :] + decay * g
            if y > 0:
                moment = moment + g
        zero = (at_row + peer * share + at_lane) == 0
        ssend[k, 0] = f
        ssend[k, 1] = jnp.where(zero, moment, g)

    def first(k):
        return pltpu.make_async_remote_copy(ssend.at[k], srecv.at[k], send1.at[k], recv1.at[k], device_id=(sim, lax.rem(me + k, slabs)), device_id_type=MESH)

    @pl.loop(1, slabs)
    def _(k):
        first(k).start()

    srecv[0] = ssend[0]

    @pl.loop(1, slabs)
    def _(k):
        first(k).wait()

    pick = pl.ds(pl.multiple_of(me * share, share), share)
    qq, wr = q[pick, :], wrap[pick, :]
    zero = (at_row + me * share + at_lane) == 0

    def slot(s):
        return lax.rem(me - s + slabs, slabs)

    acc_f = jnp.zeros(small, jnp.float32)
    acc_b = jnp.zeros(small, jnp.float32)
    lever = jnp.zeros(small, jnp.float32)
    for s in range(slabs):
        fl, bl = srecv[slot(s), 0], srecv[slot(s), 1]
        acc_f = fl + qq * acc_f
        lever = lever + ((rows * s) * fl + bl)
    for s in range(slabs - 1, -1, -1):
        acc_b = srecv[slot(s), 1] + qq * acc_b
    mean = acc_f * (1.0 / total)
    slope = (lever - mean * (0.5 * total * (total - 1))) * (1.0 / total)
    cur = jnp.where(zero, slope, acc_f * wr)
    for s in range(slabs):
        k = lax.rem(s - me + slabs, slabs)
        back[k, 0] = cur
        cur = srecv[slot(s), 0] + qq * cur - jnp.where(zero, mean * rows, 0.0)
    cur = acc_b * wr
    for s in range(slabs - 1, -1, -1):
        k = lax.rem(s - me + slabs, slabs)
        back[k, 1] = jnp.where(zero, mean, cur)
        cur = srecv[slot(s), 1] + qq * cur

    def second(k):
        return pltpu.make_async_remote_copy(back.at[k], inc.at[k], send2.at[k], recv2.at[k], device_id=(sim, lax.rem(me + k, slabs)), device_id_type=MESH)

    @pl.loop(1, slabs)
    def _(k):
        second(k).start()

    inc[0] = back[0]

    @pl.loop(1, slabs)
    def _(k):
        second(k).wait()

    @pl.loop(0, slabs)
    def _(k):
        p = lax.rem(me - k + slabs, slabs)
        pick = pl.ds(pl.multiple_of(p * share, share), share)
        decay, scale = mu[pick, :], coef[pick, :]
        f_in, b_in = inc[k, 0], inc[k, 1]
        f = f_in
        for y in range(rows):
            f = dhat[y, pick, :] + decay * f
            ph[y + 1, pick, :] = f
        ph[rows + 1, pick, :] = scale * (b_in + decay * f)
        g = b_in
        for y in range(rows - 1, -1, -1):
            d = dhat[y, pick, :]
            g = d + decay * g
            ph[y + 1, pick, :] = scale * (ph[y + 1, pick, :] + g - d)
        ph[0, pick, :] = scale * (f_in + decay * g)

    tile = (8, nz)
    zero = (lax.broadcasted_iota(jnp.int32, tile, 0) + lax.broadcasted_iota(jnp.int32, tile, 1)) == 0
    slope, mean = inc[me, 0, :8, :], inc[me, 1, :8, :]
    level = jnp.zeros(tile, jnp.float32)
    for y in range(rows + 2):
        ph[y, :8, :] = jnp.where(zero, level, ph[y, :8, :])
        level = level + slope
        if y < rows:
            slope = slope + (dhat[y, :8, :] - mean)

    @pl.loop(0, rows // 2 + 1)
    def _(k):
        a, b = transform(inv_x[...], [ph[2 * k], ph[2 * k + 1]], inv_z[...])
        for i, p in ((0, a), (1, b)):
            y = 2 * k + i
            pbuf[y, pl.ds(8, nx), :] = p
            pbuf[y, pl.ds(0, 8), :] = p[nx - 8 :]
            pbuf[y, pl.ds(nx + 8, 8), :] = p[:8]

    p_copy = pltpu.make_async_copy(pbuf, p_out, store.at[1])
    p_copy.start()
    out_copy.wait()
    p_copy.wait()


def gradient_kernel(b, p, out):
    _, rows, chunk, nz = b.shape
    base = pl.multiple_of(pl.program_id(0) * chunk, chunk)
    lane = lax.broadcasted_iota(jnp.int32, (8, 8, nz), 2)

    @pl.loop(0, chunk // 8)
    def _(g):
        at = pl.multiple_of(g * 8, 8)
        for h in range(0, rows, 8):
            ys, up, down = pl.ds(h + 1, 8), pl.ds(h + 2, 8), pl.ds(h, 8)
            xs = pl.ds(base + at + 8, 8)
            here = p[ys, xs, :]
            p_up = jnp.where(lane == nz - 1, here, pltpu.roll(here, nz - 1, 2))
            p_down = jnp.where(lane == 0, here, pltpu.roll(here, 1, 2))
            grads = (
                p[ys, pl.ds(base + at + 9, 8), :] - p[ys, pl.ds(base + at + 7, 8), :],
                p[up, xs, :] - p[down, xs, :],
                p_up - p_down,
            )
            for c, grad in enumerate(grads):
                turned = jnp.transpose(b[c, down, pl.ds(at, 8), :] - 0.5 * grad, (1, 0, 2))
                for i in range(8):
                    out[c, pl.ds(pl.multiple_of((at + i) * rows, rows) + h, 8), :] = turned[i]


def local(velocity, viscosity, turbines, fringe_start):
    sims, slabs = lax.axis_size("sim"), lax.axis_size("slab")
    _, _, nx, rows, nz = velocity.shape
    total = rows * slabs
    share = nx // slabs
    f32 = jnp.float32
    sds = lambda *s: jax.ShapeDtypeStruct(s, f32)
    vel = velocity.reshape(3, nx * rows, nz)
    visc = viscosity.reshape(nx * rows, nz)
    turb = turbines.reshape(nx * rows, nz)
    fringe = lax.dynamic_slice_in_dim(velocity[0], fringe_start[0], FR, 1)
    chunks = max(rows // 8, 1)
    cut = (chunks, 3, FR * (rows // chunks), nz)
    fringe = fringe.reshape(3, FR, chunks, rows // chunks, nz).transpose(2, 0, 1, 3, 4).reshape(cut)
    t = tables(nx, total, nz, rows)
    profile = np.sin(math.pi * (np.arange(FR) + 0.5) / FR) ** 2
    prof = np.repeat(profile[:, None], nz, 1).astype(np.float32)
    DMA = pltpu.SemaphoreType.DMA
    buf = lambda *s: VM(s, f32)
    pair = (slabs, 2, share, nz)
    scratch = [
        buf(3, nx * rows, nz), buf(nx * rows, nz), VM((nx * rows, nz), jnp.int32), buf(2, 4, nx, nz), buf(2, 4, nx, nz),
        buf(*cut), VM((nx, 3 * FR), jnp.bfloat16), buf(nx, nz), buf(4, rows + 2, nx, nz),
        buf(3, rows, nx, nz), buf(rows, nx, nz), buf(rows + 2, nx, nz), buf(rows + 2, nx + 16, nz), buf(2, nx, nz), buf(2, nx, nz), buf(2, FR, nz), buf(2, FR, nz),
        buf(*pair), buf(*pair), buf(*pair), buf(*pair),
        DMA((3,)), DMA((2,)), DMA((2,)), DMA((2,)), DMA((max(sims - 1, 1), chunks + 2)), DMA((chunks + 2,)), DMA((2,)), DMA((2,)),
    ] + [DMA((slabs,))] * 4
    blended, pressure = pl.pallas_call(
        functools.partial(main_kernel, sims, slabs),
        out_shape=(sds(3, rows, nx, nz), sds(rows + 2, nx + 16, nz)),
        in_specs=[full(pltpu.SMEM)] + [full(pl.ANY)] * 4 + [full()] * 9,
        out_specs=(full(pl.ANY), full(pl.ANY)),
        scratch_shapes=scratch,
        compiler_params=pltpu.CompilerParams(vmem_limit_bytes=GRANT, collective_id=0, has_side_effects=True),
        name="main",
    )(fringe_start, vel, visc, turb, fringe, prof, t["fwd_x"], t["fwd_z"], t["mu"], t["coef"], t["q"], t["wrap"], t["inv_x"], t["inv_z"])
    chunk = nx // 4
    out = pl.pallas_call(
        gradient_kernel,
        out_shape=sds(3, nx * rows, nz),
        grid=(nx // chunk,),
        in_specs=[
            pl.BlockSpec((3, rows, chunk, nz), lambda i: (0, 0, i, 0)),
            pl.BlockSpec((rows + 2, nx + 16, nz), lambda i: (0, 0, 0)),
        ],
        out_specs=pl.BlockSpec((3, chunk * rows, nz), lambda i: (0, i, 0)),
        compiler_params=pltpu.CompilerParams(vmem_limit_bytes=GRANT),
        name="gradient",
    )(blended, pressure)
    return out.reshape(1, 3, nx, rows, nz)


def solution(mesh):
    return jax.shard_map(
        local,
        mesh=mesh,
        in_specs=(
            P("sim", None, None, "slab", None),
            P("sim", None, "slab", None),
            P("sim", None, "slab", None),
            P(),
        ),
        out_specs=P("sim", None, None, "slab", None),
        check_vma=False,
    )
```

```python
import functools
import math

import jax
import jax.numpy as jnp
import numpy as np
from jax import lax
from jax.experimental import pallas as pl
from jax.experimental.pallas import tpu as pltpu
from jax.sharding import PartitionSpec as P

FR = 32

thrust_coef = 0.75
MESH = pl.DeviceIdType.MESH
VM = pltpu.VMEM
GRANT = 60 * 1024 * 1024


def split(value):
    high = value.astype(jnp.bfloat16)
    return high, (value - high.astype(jnp.float32)).astype(jnp.bfloat16)


def split_table(table, axis):
    high = table.astype(jnp.bfloat16)
    low = (table - high.astype(np.float32)).astype(jnp.bfloat16)
    return np.concatenate([high, high, low], axis)


def dot(a, b):
    return jnp.dot(a, b, preferred_element_type=jnp.float32)


def parts(value):
    high, rest = split(value)
    mid = value - high.astype(jnp.float32)
    low = mid - rest.astype(jnp.float32)
    return jnp.concatenate([high, rest, low.astype(jnp.bfloat16)], 0)


def along_z(value, table):
    high, low = split(value)
    return dot(jnp.concatenate([high, low, high], 1), table)


def along_x(table, value):
    high, low = split(value)
    return dot(table, jnp.concatenate([high, low, high], 0))


def transform(table_x, pair, table_z):
    nx, nz = pair[0].shape
    mid = along_z(jnp.concatenate(pair, 0), table_z)
    both = along_x(table_x, jnp.concatenate([mid[:nx], mid[nx:]], 1))
    return both[:, :nz], both[:, nz:]


def full(space=VM):
    return pl.BlockSpec(memory_space=space)


def tables(nx, ny, nz, rows):
    half = nx // 2
    wave = np.concatenate([np.arange(half), [half], np.arange(1, half)])
    at = np.arange(nx)
    angle = 2.0 * np.pi * ((wave[:, None] * at[None, :]) % nx) / nx
    is_sine = (np.arange(nx) > half)[:, None]
    fwd_x = np.where(is_sine, -np.sin(angle), np.cos(angle))
    weight = np.where((wave == 0) | (wave == half), 1.0, 2.0) / nx
    inv_x = (fwd_x * weight[:, None]).T
    m = np.arange(nz)
    cos_z = np.cos(np.pi * ((m[:, None] * (2 * m[None, :] + 1)) % (4 * nz)) / (2.0 * nz))
    inv_z = cos_z * (np.where(m == 0, 1.0, 2.0) / nz)[:, None]
    a = (4.0 * np.sin(np.pi * wave / nx) ** 2)[:, None] + (4.0 * np.sin(np.pi * m / (2.0 * nz)) ** 2)[None, :]
    root = np.sqrt(a + a * a / 4.0)
    mu = 1.0 / (1.0 + a / 2.0 + root)
    zero = a == 0.0
    coef = np.where(zero, 0.0, -1.0 / np.where(zero, 1.0, 2.0 * root))
    q = mu**rows
    wrap = 1.0 / np.where(zero, 1.0, 1.0 - mu**ny)
    f32 = lambda t: np.asarray(t, np.float32)
    return dict(fwd_x=split_table(f32(fwd_x), 1), inv_x=split_table(f32(inv_x), 1), fwd_z=split_table(f32(cos_z.T), 0), inv_z=split_table(f32(inv_z), 0), mu=f32(mu), coef=f32(coef), q=f32(q), wrap=f32(wrap))


def xroll(value, shift):
    return pltpu.roll(value, shift % value.shape[0], 0)


def zroll(value, shift):
    return pltpu.roll(value, shift % value.shape[1], 1)


def main_kernel(sims, slabs, start, vel_hbm, visc_hbm, turb_hbm, fringe, prof, fwd_x, fwd_z, mu, coef, q, wrap, inv_x, inv_z, bl_out, p_out,
                vel, visc, turb, edge, halo, pre, place, wfull, ext, bl, dhat, ph, pbuf, vh, ve, vf, pv, ssend, srecv, back, inc,
                load, store, send, recv, psend, precv, hsend, hrecv, send1, recv1, send2, recv2):
    sim, me = lax.axis_index("sim"), lax.axis_index("slab")
    after, before = lax.rem(me + 1, slabs), lax.rem(me + slabs - 1, slabs)
    rows, nx, nz = dhat.shape
    total = rows * slabs
    share = nx // slabs
    loads = [pltpu.make_async_copy(a, b, load.at[i]) for i, (a, b) in enumerate(((vel_hbm, vel), (visc_hbm, visc), (turb_hbm, turb)))]
    for copy in loads:
        copy.start()
    barrier = pltpu.get_barrier_semaphore()

    @pl.loop(1, slabs)
    def _(k):
        pl.semaphore_signal(barrier, inc=1, device_id=(sim, lax.rem(me + k, slabs)), device_id_type=MESH)

    @pl.when(sim == 0)
    def _():
        for other in range(1, sims):
            for peer in (me, after, before):
                pl.semaphore_signal(barrier, inc=1, device_id=(other, peer), device_id_type=MESH)

    @pl.when(sim != 0)
    def _():
        for peer in (me, after, before):
            pl.semaphore_signal(barrier, inc=1, device_id=(0, peer), device_id_type=MESH)

    @pl.when(sim == 0)
    def _():
        pl.semaphore_wait(barrier, slabs - 1 + 3 * (sims - 1))

    @pl.when(sim != 0)
    def _():
        pl.semaphore_wait(barrier, slabs - 1 + 3)

    chunks = fringe.shape[0]

    def give(other, j):
        return pltpu.make_async_remote_copy(fringe.at[j], pre.at[j], psend.at[other - 1, j], precv.at[j], device_id=(other, me), device_id_type=MESH)

    def give_edge(other, side):
        peer = before if side == 0 else after
        return pltpu.make_async_remote_copy(vf.at[side], pv.at[1 - side], psend.at[other - 1, chunks + side], precv.at[chunks + 1 - side], device_id=(other, peer), device_id_type=MESH)

    @pl.when(sim == 0)
    def _():
        for other in range(1, sims):
            give(other, 0).start()

    first = start[0]
    loads[0].wait()
    loads[1].wait()
    for c in range(4):
        for side, at in ((0, 0), (1, rows - 1)):
            pick = pl.ds(at, nx, stride=rows)
            edge[side, c] = visc[pick, :] if c == 3 else vel[c, pick, :]

    to_after = pltpu.make_async_remote_copy(edge.at[1], halo.at[0], send.at[0], recv.at[0], device_id=(sim, after), device_id_type=MESH)
    to_before = pltpu.make_async_remote_copy(edge.at[0], halo.at[1], send.at[1], recv.at[1], device_id=(sim, before), device_id_type=MESH)
    to_after.start()
    to_before.start()

    @pl.when(sim == 0)
    def _():
        col = lax.rem(lax.broadcasted_iota(jnp.int32, (FR, 3 * nx), 1), nx)
        at = lax.broadcasted_iota(jnp.int32, (FR, 3 * nx), 0) + first
        take = (col == at).astype(jnp.float32).astype(jnp.bfloat16)
        for side in range(2):
            vf[side] = dot(take, parts(edge[side, 1]))
            pv[side] = jnp.zeros_like(pv[side])
        for other in range(1, sims):
            for side in range(2):
                give_edge(other, side).start()
            for j in range(1, chunks):
                give(other, j).start()

    @pl.loop(0, rows)
    def _(y):
        pick = pl.ds(y, nx, stride=rows)
        for c in range(3):
            ext[c, y + 1] = vel[c, pick, :]
        ext[3, y + 1] = visc[pick, :]

    lane = lax.broadcasted_iota(jnp.int32, (nx, nz), 1)
    part = lax.broadcasted_iota(jnp.int32, place.shape, 1)
    row_of = lax.broadcasted_iota(jnp.int32, place.shape, 0) - first
    place[...] = (lax.rem(part, FR) == row_of).astype(jnp.float32).astype(jnp.bfloat16)
    wfull[...] = dot(place[...], parts(prof[...])) * (sim != 0).astype(jnp.float32)

    @pl.when(sim == 0)
    def _():
        pre[...] = jnp.zeros_like(pre)

    loads[2].wait()

    def diffuse(y):
        nu = ext[3, y + 1]
        face_x = 0.5 * (nu + xroll(nu, -1))
        face_z = jnp.where(lane == nz - 1, 0.0, 0.5 * (nu + zroll(nu, -1)))
        face_up = 0.5 * (nu + ext[3, y + 2])
        face_down = 0.5 * (nu + ext[3, y])
        for c in range(3):
            u = ext[c, y + 1]
            flux_x = face_x * (xroll(u, -1) - u)
            flux_z = face_z * (zroll(u, -1) - u)
            across_y = face_up * (ext[c, y + 2] - u) - face_down * (u - ext[c, y])
            new = u + (flux_x - xroll(flux_x, 1)) + across_y + (flux_z - zroll(flux_z, 1))
            if c == 0:
                mask = turb[pl.ds(y, nx, stride=rows), :].astype(jnp.float32)
                new = new - 0.5 * thrust_coef * mask * new * jnp.abs(new)
            bl[c, y] = new

    @pl.loop(1, rows - 1)
    def _(y):
        diffuse(y)

    to_after.wait()
    to_before.wait()
    for c in range(4):
        ext[c, 0] = halo[0, c]
        ext[c, rows + 1] = halo[1, c]

    @pl.loop(0, 2)
    def _(end):
        diffuse(end * (rows - 1))

    ve[0] = bl[1, 0]
    ve[1] = bl[1, rows - 1]

    def blend(cur, placed):
        return cur + wfull[...] * (placed - cur)

    def div(y, v_down, v_up):
        u, w = bl[0, y], bl[2, y]
        w_up = jnp.where(lane == nz - 1, w, zroll(w, -1))
        w_down = jnp.where(lane == 0, w, zroll(w, 1))
        return 0.5 * (xroll(u, -1) - xroll(u, 1)) + 0.5 * (v_up - v_down) + 0.5 * (w_up - w_down)

    v_after = pltpu.make_async_remote_copy(ve.at[1], vh.at[0], hsend.at[0], hrecv.at[0], device_id=(sim, after), device_id_type=MESH)
    v_before = pltpu.make_async_remote_copy(ve.at[0], vh.at[1], hsend.at[1], hrecv.at[1], device_id=(sim, before), device_id_type=MESH)
    part_rows = rows // chunks
    for j in range(chunks):

        @pl.when(sim != 0)
        def _():
            give(1, j).wait_recv()

        if j == 0:
            v_after.start()
            v_before.start()

        @pl.loop(0, part_rows)
        def _(i):
            y = j * part_rows + i
            rows_in = jnp.concatenate([pre[j, c, pl.ds(i, FR, stride=part_rows), :] for c in range(3)], 1)
            placed = dot(place[...], parts(rows_in))
            for c in range(3):
                bl[c, y] = blend(bl[c, y], placed[:, c * nz : (c + 1) * nz])

        @pl.loop(max(0, (part_rows // 2) * j - 1), (part_rows // 2) * (j + 1) - 1)
        def _(k):
            y = 2 * k + 1
            pair = [div(y + i, bl[1, y + i - 1], bl[1, y + i + 1]) for i in range(2)]
            dhat[y], dhat[y + 1] = transform(fwd_x[...], pair, fwd_z[...])

    out_copy = pltpu.make_async_copy(bl, bl_out, store.at[0])
    out_copy.start()
    v_after.wait()
    v_before.wait()

    @pl.when(sim != 0)
    def _():
        for side in range(2):
            give_edge(1, side).wait_recv()

    @pl.when(sim == 0)
    def _():
        for other in range(1, sims):
            for j in range(chunks):
                give(other, j).wait_send()
            for side in range(2):
                give_edge(other, side).wait_send()

    edge_rows = dot(place[...], parts(jnp.concatenate([pv[0], pv[1]], 1)))
    for side in range(2):
        vh[side] = blend(vh[side], edge_rows[:, side * nz : (side + 1) * nz])
    pair = [div(0, vh[0], bl[1, 1]), div(rows - 1, bl[1, rows - 2], vh[1])]
    dhat[0], dhat[rows - 1] = transform(fwd_x[...], pair, fwd_z[...])

    small = (share, nz)
    at_row = lax.broadcasted_iota(jnp.int32, small, 0)
    at_lane = lax.broadcasted_iota(jnp.int32, small, 1)

    def outward(k):
        return pltpu.make_async_remote_copy(ssend.at[k], srecv.at[k], send1.at[k], recv1.at[k], device_id=(sim, lax.rem(me + k, slabs)), device_id_type=MESH)

    @pl.loop(0, slabs)
    def _(k):
        peer = lax.rem(me + k, slabs)
        pick = pl.ds(pl.multiple_of(peer * share, share), share)
        decay = mu[pick, :]
        f = dhat[0, pick, :]
        for y in range(1, rows):
            f = dhat[y, pick, :] + decay * f
        g = dhat[rows - 1, pick, :]
        moment = g
        for y in range(rows - 2, -1, -1):
            g = dhat[y, pick, :] + decay * g
            if y > 0:
                moment = moment + g
        zero = (at_row + peer * share + at_lane) == 0
        ssend[k, 0] = f
        ssend[k, 1] = jnp.where(zero, moment, g)

        @pl.when(k > 1)
        def _():
            outward(k - 1).start()

    outward(slabs - 1).start()
    srecv[0] = ssend[0]

    @pl.loop(1, slabs)
    def _(k):
        outward(k).wait()

    pick = pl.ds(pl.multiple_of(me * share, share), share)
    qq, wr = q[pick, :], wrap[pick, :]
    zero = (at_row + me * share + at_lane) == 0

    def slot(s):
        return lax.rem(me - s + slabs, slabs)

    acc_f = jnp.zeros(small, jnp.float32)
    acc_b = jnp.zeros(small, jnp.float32)
    lever = jnp.zeros(small, jnp.float32)
    for s in range(slabs):
        fl, bl = srecv[slot(s), 0], srecv[slot(s), 1]
        acc_f = fl + qq * acc_f
        lever = lever + ((rows * s) * fl + bl)
    for s in range(slabs - 1, -1, -1):
        acc_b = srecv[slot(s), 1] + qq * acc_b
    mean = acc_f * (1.0 / total)
    slope = (lever - mean * (0.5 * total * (total - 1))) * (1.0 / total)
    cur = jnp.where(zero, slope, acc_f * wr)
    for s in range(slabs):
        k = lax.rem(s - me + slabs, slabs)
        back[k, 0] = cur
        cur = srecv[slot(s), 0] + qq * cur - jnp.where(zero, mean * rows, 0.0)
    cur = acc_b * wr
    for s in range(slabs - 1, -1, -1):
        k = lax.rem(s - me + slabs, slabs)
        back[k, 1] = jnp.where(zero, mean, cur)
        cur = srecv[slot(s), 1] + qq * cur

    def second(k):
        return pltpu.make_async_remote_copy(back.at[k], inc.at[k], send2.at[k], recv2.at[k], device_id=(sim, lax.rem(me + k, slabs)), device_id_type=MESH)

    @pl.loop(1, slabs)
    def _(k):
        second(k).start()

    inc[0] = back[0]

    @pl.loop(0, slabs)
    def _(k):
        @pl.when(k > 0)
        def _():
            second(k).wait()

        p = lax.rem(me - k + slabs, slabs)
        pick = pl.ds(pl.multiple_of(p * share, share), share)
        decay, scale = mu[pick, :], coef[pick, :]
        f_in, b_in = inc[k, 0], inc[k, 1]
        f = f_in
        for y in range(rows):
            f = dhat[y, pick, :] + decay * f
            ph[y + 1, pick, :] = f
        ph[rows + 1, pick, :] = scale * (b_in + decay * f)
        g = b_in
        for y in range(rows - 1, -1, -1):
            d = dhat[y, pick, :]
            g = d + decay * g
            ph[y + 1, pick, :] = scale * (ph[y + 1, pick, :] + g - d)
        ph[0, pick, :] = scale * (f_in + decay * g)

    tile = (8, nz)
    zero = (lax.broadcasted_iota(jnp.int32, tile, 0) + lax.broadcasted_iota(jnp.int32, tile, 1)) == 0
    slope, mean = inc[me, 0, :8, :], inc[me, 1, :8, :]
    level = jnp.zeros(tile, jnp.float32)
    for y in range(rows + 2):
        ph[y, :8, :] = jnp.where(zero, level, ph[y, :8, :])
        level = level + slope
        if y < rows:
            slope = slope + (dhat[y, :8, :] - mean)

    def planes(k):
        return pltpu.make_async_copy(pbuf.at[pl.ds(2 * k, 2)], p_out.at[pl.ds(2 * k, 2)], store.at[1])

    @pl.loop(0, rows // 2 + 1)
    def _(k):
        a, b = transform(inv_x[...], [ph[2 * k], ph[2 * k + 1]], inv_z[...])
        for i, p in ((0, a), (1, b)):
            y = 2 * k + i
            pbuf[y, pl.ds(8, nx), :] = p
            pbuf[y, pl.ds(0, 8), :] = p[nx - 8 :]
            pbuf[y, pl.ds(nx + 8, 8), :] = p[:8]

        @pl.when(k > 0)
        def _():
            planes(k - 1).start()

    planes(rows // 2).start()
    out_copy.wait()
    pltpu.make_async_copy(pbuf, p_out, store.at[1]).wait()


def gradient_kernel(b, p, out):
    _, rows, chunk, nz = b.shape
    base = pl.multiple_of(pl.program_id(0) * chunk, chunk)
    lane = lax.broadcasted_iota(jnp.int32, (8, 8, nz), 2)

    @pl.loop(0, chunk // 8)
    def _(g):
        at = pl.multiple_of(g * 8, 8)
        for h in range(0, rows, 8):
            ys, up, down = pl.ds(h + 1, 8), pl.ds(h + 2, 8), pl.ds(h, 8)
            xs = pl.ds(base + at + 8, 8)
            here = p[ys, xs, :]
            p_up = jnp.where(lane == nz - 1, here, pltpu.roll(here, nz - 1, 2))
            p_down = jnp.where(lane == 0, here, pltpu.roll(here, 1, 2))
            grads = (
                p[ys, pl.ds(base + at + 9, 8), :] - p[ys, pl.ds(base + at + 7, 8), :],
                p[up, xs, :] - p[down, xs, :],
                p_up - p_down,
            )
            for c, grad in enumerate(grads):
                turned = jnp.transpose(b[c, down, pl.ds(at, 8), :] - 0.5 * grad, (1, 0, 2))
                for i in range(8):
                    out[c, pl.ds(pl.multiple_of((at + i) * rows, rows) + h, 8), :] = turned[i]


def local(velocity, viscosity, turbines, fringe_start):
    sims, slabs = lax.axis_size("sim"), lax.axis_size("slab")
    _, _, nx, rows, nz = velocity.shape
    total = rows * slabs
    share = nx // slabs
    f32 = jnp.float32
    sds = lambda *s: jax.ShapeDtypeStruct(s, f32)
    vel = velocity.reshape(3, nx * rows, nz)
    visc = viscosity.reshape(nx * rows, nz)
    turb = turbines.reshape(nx * rows, nz)
    fringe = lax.dynamic_slice_in_dim(velocity[0], fringe_start[0], FR, 1)
    chunks = max(rows // 8, 1)
    cut = (chunks, 3, FR * (rows // chunks), nz)
    fringe = fringe.reshape(3, FR, chunks, rows // chunks, nz).transpose(2, 0, 1, 3, 4).reshape(cut)
    t = tables(nx, total, nz, rows)
    profile = np.sin(math.pi * (np.arange(FR) + 0.5) / FR) ** 2
    prof = np.repeat(profile[:, None], nz, 1).astype(np.float32)
    DMA = pltpu.SemaphoreType.DMA
    buf = lambda *s: VM(s, f32)
    pair = (slabs, 2, share, nz)
    scratch = [
        buf(3, nx * rows, nz), buf(nx * rows, nz), VM((nx * rows, nz), jnp.int32), buf(2, 4, nx, nz), buf(2, 4, nx, nz),
        buf(*cut), VM((nx, 3 * FR), jnp.bfloat16), buf(nx, nz), buf(4, rows + 2, nx, nz),
        buf(3, rows, nx, nz), buf(rows, nx, nz), buf(rows + 2, nx, nz), buf(rows + 2, nx + 16, nz), buf(2, nx, nz), buf(2, nx, nz), buf(2, FR, nz), buf(2, FR, nz),
        buf(*pair), buf(*pair), buf(*pair), buf(*pair),
        DMA((3,)), DMA((2,)), DMA((2,)), DMA((2,)), DMA((max(sims - 1, 1), chunks + 2)), DMA((chunks + 2,)), DMA((2,)), DMA((2,)),
    ] + [DMA((slabs,))] * 4
    blended, pressure = pl.pallas_call(
        functools.partial(main_kernel, sims, slabs),
        out_shape=(sds(3, rows, nx, nz), sds(rows + 2, nx + 16, nz)),
        in_specs=[full(pltpu.SMEM)] + [full(pl.ANY)] * 4 + [full()] * 9,
        out_specs=(full(pl.ANY), full(pl.ANY)),
        scratch_shapes=scratch,
        compiler_params=pltpu.CompilerParams(vmem_limit_bytes=GRANT, collective_id=0, has_side_effects=True),
        name="main",
    )(fringe_start, vel, visc, turb, fringe, prof, t["fwd_x"], t["fwd_z"], t["mu"], t["coef"], t["q"], t["wrap"], t["inv_x"], t["inv_z"])
    chunk = nx // 4
    out = pl.pallas_call(
        gradient_kernel,
        out_shape=sds(3, nx * rows, nz),
        grid=(nx // chunk,),
        in_specs=[
            pl.BlockSpec((3, rows, chunk, nz), lambda i: (0, 0, i, 0)),
            pl.BlockSpec((rows + 2, nx + 16, nz), lambda i: (0, 0, 0)),
        ],
        out_specs=pl.BlockSpec((3, chunk * rows, nz), lambda i: (0, i, 0)),
        compiler_params=pltpu.CompilerParams(vmem_limit_bytes=GRANT),
        name="gradient",
    )(blended, pressure)
    return out.reshape(1, 3, nx, rows, nz)


def solution(mesh):
    return jax.shard_map(
        local,
        mesh=mesh,
        in_specs=(
            P("sim", None, None, "slab", None),
            P("sim", None, "slab", None),
            P("sim", None, "slab", None),
            P(),
        ),
        out_specs=P("sim", None, None, "slab", None),
        check_vma=False,
    )
```

```python
import functools
import math

import jax
import jax.numpy as jnp
import numpy as np
from jax import lax
from jax.experimental import pallas as pl
from jax.experimental.pallas import tpu as pltpu
from jax.sharding import PartitionSpec as P

FR = 32

thrust_coef = 0.75
MESH = pl.DeviceIdType.MESH
VM = pltpu.VMEM
GRANT = 60 * 1024 * 1024


def split(value):
    high = value.astype(jnp.bfloat16)
    return high, (value - high.astype(jnp.float32)).astype(jnp.bfloat16)


def split_table(table, axis):
    high = table.astype(jnp.bfloat16)
    low = (table - high.astype(np.float32)).astype(jnp.bfloat16)
    return np.concatenate([high, high, low], axis)


def dot(a, b):
    return jnp.dot(a, b, preferred_element_type=jnp.float32)


def parts(value):
    high, rest = split(value)
    mid = value - high.astype(jnp.float32)
    low = mid - rest.astype(jnp.float32)
    return jnp.concatenate([high, rest, low.astype(jnp.bfloat16)], 0)


def along_z(value, table):
    high, low = split(value)
    return dot(jnp.concatenate([high, low, high], 1), table)


def along_x(table, value):
    high, low = split(value)
    return dot(table, jnp.concatenate([high, low, high], 0))


def transform(table_x, pair, table_z):
    nx, nz = pair[0].shape
    mid = along_z(jnp.concatenate(pair, 0), table_z)
    both = along_x(table_x, jnp.concatenate([mid[:nx], mid[nx:]], 1))
    return both[:, :nz], both[:, nz:]


def full(space=VM):
    return pl.BlockSpec(memory_space=space)


def tables(nx, ny, nz, rows):
    half = nx // 2
    wave = np.concatenate([np.arange(half), [half], np.arange(1, half)])
    at = np.arange(nx)
    angle = 2.0 * np.pi * ((wave[:, None] * at[None, :]) % nx) / nx
    is_sine = (np.arange(nx) > half)[:, None]
    fwd_x = np.where(is_sine, -np.sin(angle), np.cos(angle))
    weight = np.where((wave == 0) | (wave == half), 1.0, 2.0) / nx
    inv_x = (fwd_x * weight[:, None]).T
    m = np.arange(nz)
    cos_z = np.cos(np.pi * ((m[:, None] * (2 * m[None, :] + 1)) % (4 * nz)) / (2.0 * nz))
    inv_z = cos_z * (np.where(m == 0, 1.0, 2.0) / nz)[:, None]
    a = (4.0 * np.sin(np.pi * wave / nx) ** 2)[:, None] + (4.0 * np.sin(np.pi * m / (2.0 * nz)) ** 2)[None, :]
    root = np.sqrt(a + a * a / 4.0)
    mu = 1.0 / (1.0 + a / 2.0 + root)
    zero = a == 0.0
    coef = np.where(zero, 0.0, -1.0 / np.where(zero, 1.0, 2.0 * root))
    q = mu**rows
    wrap = 1.0 / np.where(zero, 1.0, 1.0 - mu**ny)
    f32 = lambda t: np.asarray(t, np.float32)
    return dict(fwd_x=split_table(f32(fwd_x), 1), inv_x=split_table(f32(inv_x), 1), fwd_z=split_table(f32(cos_z.T), 0), inv_z=split_table(f32(inv_z), 0), mu=f32(mu), coef=f32(coef), q=f32(q), wrap=f32(wrap))


def xroll(value, shift):
    return pltpu.roll(value, shift % value.shape[0], 0)


def zroll(value, shift):
    return pltpu.roll(value, shift % value.shape[1], 1)


def main_kernel(sims, slabs, start, vel_hbm, visc_hbm, turb_hbm, fringe, prof, fwd_x, fwd_z, mu, coef, q, wrap, inv_x, inv_z, bl_out, p_out,
                vel, visc, turb, edge, halo, pre, place, wfull, ext, bl, dhat, ph, pbuf, vh, ve, vf, pv, ssend, srecv, back, inc,
                load, store, send, recv, psend, precv, hsend, hrecv, send1, recv1, send2, recv2):
    sim, me = lax.axis_index("sim"), lax.axis_index("slab")
    after, before = lax.rem(me + 1, slabs), lax.rem(me + slabs - 1, slabs)
    rows, nx, nz = dhat.shape
    total = rows * slabs
    share = nx // slabs
    loads = [pltpu.make_async_copy(a, b, load.at[i]) for i, (a, b) in enumerate(((vel_hbm, vel), (visc_hbm, visc), (turb_hbm, turb)))]
    for copy in loads:
        copy.start()
    barrier = pltpu.get_barrier_semaphore()

    @pl.loop(1, slabs)
    def _(k):
        pl.semaphore_signal(barrier, inc=1, device_id=(sim, lax.rem(me + k, slabs)), device_id_type=MESH)

    @pl.when(sim == 0)
    def _():
        for other in range(1, sims):
            for peer in (me, after, before):
                pl.semaphore_signal(barrier, inc=1, device_id=(other, peer), device_id_type=MESH)

    @pl.when(sim != 0)
    def _():
        for peer in (me, after, before):
            pl.semaphore_signal(barrier, inc=1, device_id=(0, peer), device_id_type=MESH)

    @pl.when(sim == 0)
    def _():
        pl.semaphore_wait(barrier, slabs - 1 + 3 * (sims - 1))

    @pl.when(sim != 0)
    def _():
        pl.semaphore_wait(barrier, slabs - 1 + 3)

    chunks = fringe.shape[0]

    def give(other, j):
        return pltpu.make_async_remote_copy(fringe.at[j], pre.at[j], psend.at[other - 1, j], precv.at[j], device_id=(other, me), device_id_type=MESH)

    def give_edge(other, side):
        peer = before if side == 0 else after
        return pltpu.make_async_remote_copy(vf.at[side], pv.at[1 - side], psend.at[other - 1, chunks + side], precv.at[chunks + 1 - side], device_id=(other, peer), device_id_type=MESH)

    @pl.when(sim == 0)
    def _():
        for other in range(1, sims):
            give(other, 0).start()

    first = start[0]
    loads[0].wait()
    loads[1].wait()
    for c in range(4):
        for side, at in ((0, 0), (1, rows - 1)):
            pick = pl.ds(at, nx, stride=rows)
            edge[side, c] = visc[pick, :] if c == 3 else vel[c, pick, :]

    to_after = pltpu.make_async_remote_copy(edge.at[1], halo.at[0], send.at[0], recv.at[0], device_id=(sim, after), device_id_type=MESH)
    to_before = pltpu.make_async_remote_copy(edge.at[0], halo.at[1], send.at[1], recv.at[1], device_id=(sim, before), device_id_type=MESH)
    to_after.start()
    to_before.start()

    @pl.when(sim == 0)
    def _():
        col = lax.rem(lax.broadcasted_iota(jnp.int32, (FR, 3 * nx), 1), nx)
        at = lax.broadcasted_iota(jnp.int32, (FR, 3 * nx), 0) + first
        take = (col == at).astype(jnp.float32).astype(jnp.bfloat16)
        for side in range(2):
            vf[side] = dot(take, parts(edge[side, 1]))
            pv[side] = jnp.zeros_like(pv[side])
        for other in range(1, sims):
            for side in range(2):
                give_edge(other, side).start()
            for j in range(1, chunks):
                give(other, j).start()

    @pl.loop(0, rows)
    def _(y):
        pick = pl.ds(y, nx, stride=rows)
        for c in range(3):
            ext[c, y + 1] = vel[c, pick, :]
        ext[3, y + 1] = visc[pick, :]

    lane = lax.broadcasted_iota(jnp.int32, (nx, nz), 1)
    part = lax.broadcasted_iota(jnp.int32, place.shape, 1)
    row_of = lax.broadcasted_iota(jnp.int32, place.shape, 0) - first
    place[...] = (lax.rem(part, FR) == row_of).astype(jnp.float32).astype(jnp.bfloat16)
    wfull[...] = dot(place[...], parts(prof[...])) * (sim != 0).astype(jnp.float32)

    @pl.when(sim == 0)
    def _():
        pre[...] = jnp.zeros_like(pre)

    loads[2].wait()

    def diffuse(y):
        nu = ext[3, y + 1]
        face_x = 0.5 * (nu + xroll(nu, -1))
        face_z = jnp.where(lane == nz - 1, 0.0, 0.5 * (nu + zroll(nu, -1)))
        face_up = 0.5 * (nu + ext[3, y + 2])
        face_down = 0.5 * (nu + ext[3, y])
        for c in range(3):
            u = ext[c, y + 1]
            flux_x = face_x * (xroll(u, -1) - u)
            flux_z = face_z * (zroll(u, -1) - u)
            across_y = face_up * (ext[c, y + 2] - u) - face_down * (u - ext[c, y])
            new = u + (flux_x - xroll(flux_x, 1)) + across_y + (flux_z - zroll(flux_z, 1))
            if c == 0:
                mask = turb[pl.ds(y, nx, stride=rows), :].astype(jnp.float32)
                new = new - 0.5 * thrust_coef * mask * new * jnp.abs(new)
            bl[c, y] = new

    @pl.loop(1, rows - 1)
    def _(y):
        diffuse(y)

    to_after.wait()
    to_before.wait()
    for c in range(4):
        ext[c, 0] = halo[0, c]
        ext[c, rows + 1] = halo[1, c]

    @pl.loop(0, 2)
    def _(end):
        diffuse(end * (rows - 1))

    ve[0] = bl[1, 0]
    ve[1] = bl[1, rows - 1]

    def blend(cur, placed):
        return cur + wfull[...] * (placed - cur)

    def div(y, v_down, v_up):
        u, w = bl[0, y], bl[2, y]
        w_up = jnp.where(lane == nz - 1, w, zroll(w, -1))
        w_down = jnp.where(lane == 0, w, zroll(w, 1))
        return 0.5 * (xroll(u, -1) - xroll(u, 1)) + 0.5 * (v_up - v_down) + 0.5 * (w_up - w_down)

    v_after = pltpu.make_async_remote_copy(ve.at[1], vh.at[0], hsend.at[0], hrecv.at[0], device_id=(sim, after), device_id_type=MESH)
    v_before = pltpu.make_async_remote_copy(ve.at[0], vh.at[1], hsend.at[1], hrecv.at[1], device_id=(sim, before), device_id_type=MESH)
    part_rows = rows // chunks
    for j in range(chunks):

        @pl.when(sim != 0)
        def _():
            give(1, j).wait_recv()

        if j == 0:
            v_after.start()
            v_before.start()

        @pl.loop(0, part_rows)
        def _(i):
            y = j * part_rows + i
            rows_in = jnp.concatenate([pre[j, c, pl.ds(i, FR, stride=part_rows), :] for c in range(3)], 1)
            placed = dot(place[...], parts(rows_in))
            for c in range(3):
                bl[c, y] = blend(bl[c, y], placed[:, c * nz : (c + 1) * nz])

        @pl.loop(max(0, (part_rows // 2) * j - 1), (part_rows // 2) * (j + 1) - 1)
        def _(k):
            y = 2 * k + 1
            pair = [div(y + i, bl[1, y + i - 1], bl[1, y + i + 1]) for i in range(2)]
            dhat[y], dhat[y + 1] = transform(fwd_x[...], pair, fwd_z[...])

    out_copy = pltpu.make_async_copy(bl, bl_out, store.at[0])
    out_copy.start()
    v_after.wait()
    v_before.wait()

    @pl.when(sim != 0)
    def _():
        for side in range(2):
            give_edge(1, side).wait_recv()

    @pl.when(sim == 0)
    def _():
        for other in range(1, sims):
            for j in range(chunks):
                give(other, j).wait_send()
            for side in range(2):
                give_edge(other, side).wait_send()

    edge_rows = dot(place[...], parts(jnp.concatenate([pv[0], pv[1]], 1)))
    for side in range(2):
        vh[side] = blend(vh[side], edge_rows[:, side * nz : (side + 1) * nz])
    pair = [div(0, vh[0], bl[1, 1]), div(rows - 1, bl[1, rows - 2], vh[1])]
    dhat[0], dhat[rows - 1] = transform(fwd_x[...], pair, fwd_z[...])

    small = (share, nz)
    at_row = lax.broadcasted_iota(jnp.int32, small, 0)
    at_lane = lax.broadcasted_iota(jnp.int32, small, 1)

    def outward(k):
        return pltpu.make_async_remote_copy(ssend.at[k], srecv.at[k], send1.at[k], recv1.at[k], device_id=(sim, lax.rem(me + k, slabs)), device_id_type=MESH)

    @pl.loop(0, slabs)
    def _(k):
        peer = lax.rem(me + k, slabs)
        pick = pl.ds(pl.multiple_of(peer * share, share), share)
        decay = mu[pick, :]
        f = dhat[0, pick, :]
        for y in range(1, rows):
            f = dhat[y, pick, :] + decay * f
        g = dhat[rows - 1, pick, :]
        moment = g
        for y in range(rows - 2, -1, -1):
            g = dhat[y, pick, :] + decay * g
            if y > 0:
                moment = moment + g
        zero = (at_row + peer * share + at_lane) == 0
        ssend[k, 0] = f
        ssend[k, 1] = jnp.where(zero, moment, g)

        @pl.when(k > 1)
        def _():
            outward(k - 1).start()

    outward(slabs - 1).start()
    srecv[0] = ssend[0]

    @pl.loop(1, slabs)
    def _(k):
        outward(k).wait()

    pick = pl.ds(pl.multiple_of(me * share, share), share)
    qq, wr = q[pick, :], wrap[pick, :]
    zero = (at_row + me * share + at_lane) == 0

    def slot(s):
        return lax.rem(me - s + slabs, slabs)

    acc_f = jnp.zeros(small, jnp.float32)
    acc_b = jnp.zeros(small, jnp.float32)
    lever = jnp.zeros(small, jnp.float32)
    for s in range(slabs):
        fl, bl = srecv[slot(s), 0], srecv[slot(s), 1]
        acc_f = fl + qq * acc_f
        lever = lever + ((rows * s) * fl + bl)
    for s in range(slabs - 1, -1, -1):
        acc_b = srecv[slot(s), 1] + qq * acc_b
    mean = acc_f * (1.0 / total)
    slope = (lever - mean * (0.5 * total * (total - 1))) * (1.0 / total)
    cur = jnp.where(zero, slope, acc_f * wr)
    for s in range(slabs):
        k = lax.rem(s - me + slabs, slabs)
        back[k, 0] = cur
        cur = srecv[slot(s), 0] + qq * cur - jnp.where(zero, mean * rows, 0.0)
    cur = acc_b * wr
    for s in range(slabs - 1, -1, -1):
        k = lax.rem(s - me + slabs, slabs)
        back[k, 1] = jnp.where(zero, mean, cur)
        cur = srecv[slot(s), 1] + qq * cur

    def second(k):
        return pltpu.make_async_remote_copy(back.at[k], inc.at[k], send2.at[k], recv2.at[k], device_id=(sim, lax.rem(me + k, slabs)), device_id_type=MESH)

    @pl.loop(1, slabs)
    def _(k):
        second(k).start()

    inc[0] = back[0]

    @pl.loop(0, slabs)
    def _(k):
        @pl.when(k > 0)
        def _():
            second(k).wait()

        p = lax.rem(me - k + slabs, slabs)
        pick = pl.ds(pl.multiple_of(p * share, share), share)
        decay, scale = mu[pick, :], coef[pick, :]
        f_in, b_in = inc[k, 0], inc[k, 1]
        f = f_in
        for y in range(rows):
            f = dhat[y, pick, :] + decay * f
            ph[y + 1, pick, :] = f
        ph[rows + 1, pick, :] = scale * (b_in + decay * f)
        g = b_in
        for y in range(rows - 1, -1, -1):
            d = dhat[y, pick, :]
            g = d + decay * g
            ph[y + 1, pick, :] = scale * (ph[y + 1, pick, :] + g - d)
        ph[0, pick, :] = scale * (f_in + decay * g)

    tile = (8, nz)
    zero = (lax.broadcasted_iota(jnp.int32, tile, 0) + lax.broadcasted_iota(jnp.int32, tile, 1)) == 0
    slope, mean = inc[me, 0, :8, :], inc[me, 1, :8, :]
    level = jnp.zeros(tile, jnp.float32)
    for y in range(rows + 2):
        ph[y, :8, :] = jnp.where(zero, level, ph[y, :8, :])
        level = level + slope
        if y < rows:
            slope = slope + (dhat[y, :8, :] - mean)

    def planes(k):
        return pltpu.make_async_copy(pbuf.at[pl.ds(2 * k, 2)], p_out.at[pl.ds(2 * k, 2)], store.at[1])

    @pl.loop(0, rows // 2 + 1)
    def _(k):
        a, b = transform(inv_x[...], [ph[2 * k], ph[2 * k + 1]], inv_z[...])
        for i, p in ((0, a), (1, b)):
            y = 2 * k + i
            pbuf[y, pl.ds(8, nx), :] = p
            pbuf[y, pl.ds(0, 8), :] = p[nx - 8 :]
            pbuf[y, pl.ds(nx + 8, 8), :] = p[:8]

        @pl.when(k > 0)
        def _():
            planes(k - 1).start()

    planes(rows // 2).start()
    out_copy.wait()
    pltpu.make_async_copy(pbuf, p_out, store.at[1]).wait()


def gradient_kernel(b, p, out):
    _, rows, chunk, nz = b.shape
    base = pl.multiple_of(pl.program_id(0) * chunk, chunk)
    lane = lax.broadcasted_iota(jnp.int32, (8, 8, nz), 2)

    @pl.loop(0, chunk // 8)
    def _(g):
        at = pl.multiple_of(g * 8, 8)
        for h in range(0, rows, 8):
            ys, up, down = pl.ds(h + 1, 8), pl.ds(h + 2, 8), pl.ds(h, 8)
            xs = pl.ds(pl.multiple_of(base + at + 8, 8), 8)
            here = p[ys, xs, :]
            p_up = jnp.where(lane == nz - 1, here, pltpu.roll(here, nz - 1, 2))
            p_down = jnp.where(lane == 0, here, pltpu.roll(here, 1, 2))
            grads = (
                p[ys, pl.ds(base + at + 9, 8), :] - p[ys, pl.ds(base + at + 7, 8), :],
                p[up, xs, :] - p[down, xs, :],
                p_up - p_down,
            )
            for c, grad in enumerate(grads):
                turned = jnp.transpose(b[c, down, pl.ds(at, 8), :] - 0.5 * grad, (1, 0, 2))
                for i in range(8):
                    out[c, pl.ds(pl.multiple_of((at + i) * rows, rows) + h, 8), :] = turned[i]


def local(velocity, viscosity, turbines, fringe_start):
    sims, slabs = lax.axis_size("sim"), lax.axis_size("slab")
    _, _, nx, rows, nz = velocity.shape
    total = rows * slabs
    share = nx // slabs
    f32 = jnp.float32
    sds = lambda *s: jax.ShapeDtypeStruct(s, f32)
    vel = velocity.reshape(3, nx * rows, nz)
    visc = viscosity.reshape(nx * rows, nz)
    turb = turbines.reshape(nx * rows, nz)
    fringe = lax.dynamic_slice_in_dim(velocity[0], fringe_start[0], FR, 1)
    chunks = max(rows // 8, 1)
    cut = (chunks, 3, FR * (rows // chunks), nz)
    fringe = fringe.reshape(3, FR, chunks, rows // chunks, nz).transpose(2, 0, 1, 3, 4).reshape(cut)
    t = tables(nx, total, nz, rows)
    profile = np.sin(math.pi * (np.arange(FR) + 0.5) / FR) ** 2
    prof = np.repeat(profile[:, None], nz, 1).astype(np.float32)
    DMA = pltpu.SemaphoreType.DMA
    buf = lambda *s: VM(s, f32)
    pair = (slabs, 2, share, nz)
    scratch = [
        buf(3, nx * rows, nz), buf(nx * rows, nz), VM((nx * rows, nz), jnp.int32), buf(2, 4, nx, nz), buf(2, 4, nx, nz),
        buf(*cut), VM((nx, 3 * FR), jnp.bfloat16), buf(nx, nz), buf(4, rows + 2, nx, nz),
        buf(3, rows, nx, nz), buf(rows, nx, nz), buf(rows + 2, nx, nz), buf(rows + 2, nx + 16, nz), buf(2, nx, nz), buf(2, nx, nz), buf(2, FR, nz), buf(2, FR, nz),
        buf(*pair), buf(*pair), buf(*pair), buf(*pair),
        DMA((3,)), DMA((2,)), DMA((2,)), DMA((2,)), DMA((max(sims - 1, 1), chunks + 2)), DMA((chunks + 2,)), DMA((2,)), DMA((2,)),
    ] + [DMA((slabs,))] * 4
    blended, pressure = pl.pallas_call(
        functools.partial(main_kernel, sims, slabs),
        out_shape=(sds(3, rows, nx, nz), sds(rows + 2, nx + 16, nz)),
        in_specs=[full(pltpu.SMEM)] + [full(pl.ANY)] * 4 + [full()] * 9,
        out_specs=(full(pl.ANY), full(pl.ANY)),
        scratch_shapes=scratch,
        compiler_params=pltpu.CompilerParams(vmem_limit_bytes=GRANT, collective_id=0, has_side_effects=True),
        name="main",
    )(fringe_start, vel, visc, turb, fringe, prof, t["fwd_x"], t["fwd_z"], t["mu"], t["coef"], t["q"], t["wrap"], t["inv_x"], t["inv_z"])
    chunk = nx // 4
    out = pl.pallas_call(
        gradient_kernel,
        out_shape=sds(3, nx * rows, nz),
        grid=(nx // chunk,),
        in_specs=[
            pl.BlockSpec((3, rows, chunk, nz), lambda i: (0, 0, i, 0)),
            pl.BlockSpec((rows + 2, nx + 16, nz), lambda i: (0, 0, 0)),
        ],
        out_specs=pl.BlockSpec((3, chunk * rows, nz), lambda i: (0, i, 0)),
        compiler_params=pltpu.CompilerParams(vmem_limit_bytes=GRANT),
        name="gradient",
    )(blended, pressure)
    return out.reshape(1, 3, nx, rows, nz)


def solution(mesh):
    return jax.shard_map(
        local,
        mesh=mesh,
        in_specs=(
            P("sim", None, None, "slab", None),
            P("sim", None, "slab", None),
            P("sim", None, "slab", None),
            P(),
        ),
        out_specs=P("sim", None, None, "slab", None),
        check_vma=False,
    )
```
